128 devices in a mesh: bead: 2 (over core), space: 64 (over z, y, x).
Axes of the slice: x: 4, y: 4, z: 4, core: 2. Of those that a mesh axis runs over, the one named last changes fastest.
Arguments:
- positions: float32 [32, 3, 65536], P('bead', None, 'space'), may hold values from -6 to 6
- momenta: float32 [32, 3, 65536], P('bead', None, 'space'), may hold values from -6 to 6
- thermostat: float32 [32, 8, 3, 65536], P('bead', None, None, 'space'), may hold values from -6 to 6
- white_noise: float32 [32, 9, 3, 65536], P('bead', None, None, 'space'), may hold values from -6 to 6
- drift_matrix: float32 [32, 9, 9], P('bead'), may hold values from -2 to 2
- noise_matrix: float32 [32, 9, 9], P('bead'), may hold values from -2 to 2
- leave_up: int32 [512], P('space'), may hold values from 0 to 1023, as said below
- leave_down: int32 [512], P('space'), may hold values from 0 to 1023, as said below
- ghost_up: int32 [32768], P('space'), may hold values from 0 to 1023, as said below
- ghost_down: int32 [32768], P('space'), may hold values from 0 to 1023, as said below
- neighbours: int32 [32, 65536], P(None, 'space'), may hold values from 0 to 2047, as said below
Outputs:
- moved_positions: float32 [32, 3, 65536], P('bead', None, 'space')
- moved_momenta: float32 [32, 3, 65536], P('bead', None, 'space')
- moved_thermostat: float32 [32, 8, 3, 65536], P('bead', None, None, 'space')
The draws below stay inside these ranges and needn't reach their ends.
Inputs may be any that keep to these rules, and one draw needn't show every extreme that they name: Within one slab the 8 rows of leave_up and the 8 rows of leave_down are all distinct; together they are a small share of the slab. Within one slab the rows of leave_down are distinct and none of them is in leave_up. Within one slab the rows of ghost_up are distinct, and together with ghost_down they name every row of the slab once. Within one slab the rows of ghost_down are distinct and none of them is in ghost_up. `neighbours`: an entry equal to the atom's own local row is an empty slot, contributing nothing; in each slab some atom uses all 32 slots.
All inputs are finite; a program needn't handle non-finite values.
Results may differ from the reference program's by a relative error of at most 0.000086.
Values sent between devices are 32-bit elements; how exact they have to be, the bound alone decides.
No kernel may reach another device: no remote copies, remote signals or barrier semaphores. Data moves between devices by JAX's collectives and lax.ppermute only.
A program may use at most 256 MiB of HBM per device.

```python
import math
import jax
import jax.numpy as jnp
from jax import lax

BEADS = 32
STATES = 9
ATOM_DEV = 1024
SLOTS = 32
MIG = 8
GHOST = 512
NATOM = 65536
N_SPACE = 64


def slab_orders(key, seed_tag):
    slab_count = NATOM // ATOM_DEV
    keys = jax.random.split(jax.random.fold_in(key, seed_tag), slab_count)
    return jax.vmap(lambda single: jax.random.permutation(single, ATOM_DEV))(keys).astype(jnp.int32)


def draw_leave_up(key, part):
    return slab_orders(key, 11)[:, :MIG].reshape(-1)


def draw_leave_down(key, part):
    return slab_orders(key, 11)[:, MIG:2 * MIG].reshape(-1)


def draw_ghost_up(key, part):
    return slab_orders(key, 23)[:, :GHOST].reshape(-1)


def draw_ghost_down(key, part):
    return slab_orders(key, 23)[:, GHOST:2 * GHOST].reshape(-1)


def draw_neighbours(key, part):
    table_rows = ATOM_DEV + 2 * GHOST
    stride = (table_rows - 1) // SLOTS
    first_key, second_key = jax.random.split(jax.random.fold_in(key, 37))
    slot_index = jnp.arange(SLOTS, dtype=jnp.int32)[:, None]
    local_row = (jnp.arange(NATOM, dtype=jnp.int32) % ATOM_DEV)[None, :]
    slab_index = (jnp.arange(NATOM, dtype=jnp.int32) // ATOM_DEV)[None, :]
    jitter = jax.random.randint(first_key, (SLOTS, NATOM), 0, stride)
    reach = 1 + slot_index * stride + jitter
    reach = jnp.where((local_row == 0) & (slot_index == 0), table_rows - 1, reach)
    partner = (local_row + reach) % table_rows
    limit = jnp.where(slab_index % 4 == 0, SLOTS, SLOTS // 2)
    counts = jnp.minimum(jax.random.randint(second_key, (1, NATOM), 1, SLOTS + 1), limit)
    counts = jnp.where(local_row == 0, SLOTS - 1, jnp.where(local_row == 1, SLOTS, counts))
    return jnp.where(slot_index < counts, partner, local_row).astype(jnp.int32)


def block_levels(rng, extent, cuts, least, largest):
    level, own = 1.0, jax.random.fold_in(rng, 6)
    for axis_at, blocks in cuts:
        draws = jnp.exp(jax.random.uniform(jax.random.fold_in(own, axis_at), (blocks,), jnp.float32, least / len(cuts), largest / len(cuts)))
        level = level * jnp.repeat(draws, extent[axis_at] // blocks).reshape([-1 if axis == axis_at else 1 for axis in range(len(extent))])
    return level


def bell_draw(key, shape, deviation, bound, shards=(), kind=jnp.bfloat16):
    gain = block_levels(key, shape, shards, -0.22, 0.18) if shards else 1.0
    array = jax.random.normal(key, shape, jnp.float32) * deviation * gain
    return jnp.minimum(jnp.maximum(array, -bound), bound).astype(kind)


def setup_inputs(seed: int = 0) -> dict:
    streams_of = jax.random.split(jax.random.key(seed), 12)
    positions = bell_draw(streams_of[0], (BEADS, 3, NATOM), 1.0, 6.0, ((0, 2), (2, 64)), jnp.float32)
    momenta = bell_draw(streams_of[1], (BEADS, 3, NATOM), 1.0, 6.0, ((0, 2), (2, 64)), jnp.float32)
    thermostat = bell_draw(streams_of[2], (BEADS, STATES - 1, 3, NATOM), 1.0, 6.0, ((0, 2), (3, 64)), jnp.float32)
    white_noise = bell_draw(streams_of[3], (BEADS, STATES, 3, NATOM), 1.0, 6.0, ((0, 2), (3, 64)), jnp.float32)
    drift_matrix = bell_draw(streams_of[4], (BEADS, STATES, STATES), STATES ** -0.5, 2.0, ((0, 2),), jnp.float32)
    noise_matrix = bell_draw(streams_of[5], (BEADS, STATES, STATES), STATES ** -0.5, 2.0, ((0, 2),), jnp.float32)
    leave_up = draw_leave_up(jax.random.fold_in(streams_of[11], 71), 0)
    leave_down = draw_leave_down(jax.random.fold_in(streams_of[11], 71), 0)
    ghost_up = draw_ghost_up(jax.random.fold_in(streams_of[11], 71), 0)
    ghost_down = draw_ghost_down(jax.random.fold_in(streams_of[11], 71), 0)
    neighbours = draw_neighbours(jax.random.fold_in(streams_of[11], 71), 0)
    return dict(positions=positions, momenta=momenta, thermostat=thermostat, white_noise=white_noise, drift_matrix=drift_matrix, noise_matrix=noise_matrix, leave_up=leave_up, leave_down=leave_down, ghost_up=ghost_up, ghost_down=ghost_down, neighbours=neighbours)


cycle_rate = 0.8
kick_scale = 0.2
core_width = 4.0

def mode_basis(beads):
    modes = jnp.arange(beads, dtype=jnp.float32)[:, None]
    sites = jnp.arange(beads, dtype=jnp.float32)[None, :]
    angles = 2.0 * math.pi * modes * sites / beads
    cosine = math.sqrt(2.0 / beads) * jnp.cos(angles)
    sine = math.sqrt(2.0 / beads) * jnp.sin(angles)
    edge = jnp.cos(angles) / math.sqrt(beads)
    centre = jnp.full_like(angles, 1.0 / math.sqrt(beads))
    middle = beads // 2
    return jnp.where(modes == 0, centre, jnp.where(modes < middle, cosine, jnp.where(modes == middle, edge, sine)))

def cycle_tables(beads):
    frequency = 2.0 * cycle_rate * jnp.sin(math.pi * jnp.arange(beads, dtype=jnp.float32) / beads)
    nonzero = jnp.where(frequency > 0, frequency, 1.0)
    sine_ratio = jnp.where(frequency > 0, jnp.sin(frequency) / nonzero, 1.0)
    return (jnp.cos(frequency), sine_ratio, frequency * jnp.sin(frequency))

def pair_forces(own, gathered):
    offset = own[..., :, None, :] - gathered
    weight = jnp.exp(-lax.optimization_barrier(jnp.sum(offset * offset, axis=-3)) / (2.0 * core_width))
    return lax.optimization_barrier(jnp.sum(offset * weight[..., None, :, :], axis=-2))

def reference(positions, momenta, thermostat, white_noise, drift_matrix, noise_matrix, leave_up, leave_down, ghost_up, ghost_down, neighbours):
    highest = lax.Precision.HIGHEST
    basis = mode_basis(BEADS)
    mode_pos = jnp.einsum('kb,bcn->kcn', basis, positions, precision=highest)
    mode_mom = jnp.einsum('kb,bcn->kcn', basis, momenta, precision=highest)
    extended = jnp.concatenate([mode_mom[:, None], thermostat], axis=1)
    evolved = jnp.einsum('kij,kjcn->kicn', drift_matrix, extended, precision=highest) + jnp.einsum('kij,kjcn->kicn', noise_matrix, white_noise, precision=highest)
    cosine, sine_ratio, stiffness = cycle_tables(BEADS)
    kicked = evolved[:, 0]
    free_pos = cosine[:, None, None] * mode_pos + sine_ratio[:, None, None] * kicked
    free_mom = cosine[:, None, None] * kicked - stiffness[:, None, None] * mode_pos
    bead_pos = jnp.einsum('kb,kcn->bcn', basis, free_pos, precision=highest)
    bead_mom = jnp.einsum('kb,kcn->bcn', basis, free_mom, precision=highest)
    new_aux = evolved[:, 1:]
    slab_base = (jnp.arange(N_SPACE, dtype=jnp.int32) * ATOM_DEV)[:, None]
    going_up = slab_base + leave_up.reshape(N_SPACE, MIG)
    going_down = slab_base + leave_down.reshape(N_SPACE, MIG)
    placing = jnp.arange(NATOM, dtype=jnp.int32)
    placing = placing.at[going_up.reshape(-1)].set(jnp.roll(going_down, -1, axis=0).reshape(-1))
    placing = placing.at[going_down.reshape(-1)].set(jnp.roll(going_up, 1, axis=0).reshape(-1))
    moved_pos = bead_pos[:, :, placing]
    slab_mom = bead_mom[:, :, placing]
    moved_aux = new_aux[:, :, :, placing]
    ghosts_low = jnp.roll(slab_base + ghost_up.reshape(N_SPACE, GHOST), 1, axis=0)
    ghosts_high = jnp.roll(slab_base + ghost_down.reshape(N_SPACE, GHOST), -1, axis=0)
    own_rows = slab_base + jnp.arange(ATOM_DEV, dtype=jnp.int32)[None, :]
    slab_table = jnp.concatenate([own_rows, ghosts_low, ghosts_high], axis=1)
    slab_ids = (jnp.arange(NATOM, dtype=jnp.int32) // ATOM_DEV)[None, :]
    partners = slab_table[slab_ids, neighbours]

    def one_bead(single):
        return pair_forces(single, single[:, partners])
    forces = lax.map(one_bead, moved_pos)
    return (moved_pos, slab_mom + kick_scale * forces, moved_aux)
```

```python
import functools
import math

import jax
import jax.numpy as jnp
import numpy as np
from jax import lax
from jax.experimental import pallas as pl
from jax.experimental.pallas import tpu as pltpu
from jax.sharding import PartitionSpec as P


BEADS = 32
HALF = 16
ATOMS = 1024
TILES = 8
SLOTS = 32
GHOST_TILES = 4
LANES = 128
FAST = 3
CHUNK = 8

cycle_rate = 0.8
kick_scale = 0.2
core_width = 4.0

F32 = jnp.float32
I32 = jnp.int32
VMEM = pl.BlockSpec(memory_space=pltpu.VMEM)
SMEM = pl.BlockSpec(memory_space=pltpu.SMEM)
ANY = pl.BlockSpec(memory_space=pl.ANY)
HBM = pl.BlockSpec(memory_space=pltpu.HBM)
HIGHEST = lax.Precision.HIGHEST


def constants():
    k = np.arange(BEADS)[:, None].astype(np.float64)
    b = np.arange(BEADS)[None, :].astype(np.float64)
    angle = 2.0 * math.pi * ((k * b) % BEADS) / BEADS
    scale = math.sqrt(2.0 / BEADS)
    basis = np.where(k < BEADS // 2, scale * np.cos(angle), scale * np.sin(angle))
    basis = np.where(k == 0, 1.0 / math.sqrt(BEADS), basis)
    basis = np.where(k == BEADS // 2, np.cos(math.pi * b) / math.sqrt(BEADS), basis)
    w = 2.0 * cycle_rate * np.sin(math.pi * np.arange(BEADS) / BEADS)
    ratio = np.where(w > 0, np.sin(w) / np.where(w > 0, w, 1.0), 1.0)
    columns = np.stack([np.cos(w), ratio, w * np.sin(w)], axis=1)
    forward, backward, tables = [], [], []
    for core in range(2):
        order = np.roll(np.arange(BEADS), -HALF * core)
        forward.append(basis[order][:, order])
        backward.append(basis[order][:, order[:HALF]].T)
        tables.append(np.pad(columns[order], ((0, 0), (0, 5))))
    tables = [np.pad(x, ((0, 0), (0, BEADS - 8))) for x in tables]
    parts = [np.concatenate(x, axis=0) for x in zip(forward, backward, tables)]
    return np.stack(parts).astype(np.float32)


CONSTANTS = constants()


def call(body, outs, args, specs=None, out_specs=None, scratch=(), flops=0, nbytes=0, limit=24, alias=None):
    return pl.pallas_call(
        body,
        out_shape=outs,
        in_specs=specs or [VMEM] * len(args),
        out_specs=out_specs or [VMEM] * len(outs),
        scratch_shapes=scratch,
        input_output_aliases=alias or {},
        compiler_params=pltpu.CompilerParams(vmem_limit_bytes=limit << 20),
        cost_estimate=pl.CostEstimate(flops=flops, bytes_accessed=nbytes, transcendentals=0),
    )(*args)


def struct(*shape, dtype=F32):
    return jax.ShapeDtypeStruct(shape, dtype)


def shifted(array, axis, by):
    devices = lax.axis_size(axis)
    return lax.ppermute(array, axis, [(i, (i + by) % devices) for i in range(devices)])


def take(values, lanes):
    return lax.gather(
        values,
        lanes[..., None],
        lax.GatherDimensionNumbers(
            offset_dims=(),
            collapsed_slice_dims=(1,),
            start_index_map=(1,),
            operand_batching_dims=(0,),
            start_indices_batching_dims=(0,),
        ),
        slice_sizes=(1, 1),
        mode=lax.GatherScatterMode.PROMISE_IN_BOUNDS,
    )


def spread(row):
    return jnp.broadcast_to(row, (8, LANES))


def cols(tile):
    if isinstance(tile, int):
        return pl.ds(tile * LANES, LANES)
    return pl.ds(pl.multiple_of(tile * LANES, LANES), LANES)


def leavers(up_ref, down_ref):
    place = lax.broadcasted_iota(I32, (8, LANES), 1) & 15
    index = jnp.zeros((8, LANES), I32)
    for j in range(8):
        index = jnp.where(place == j, up_ref[j], index)
        index = jnp.where(place == 8 + j, down_ref[j], index)
    return index


def columns_of(drift_ref, noisem_ref, k):
    out = []
    for ref in (drift_ref, noisem_ref):
        block = ref[pl.ds(HALF + k, 8, stride=HALF), :]
        out += [jnp.broadcast_to(block[:, j:j + 1], (8, LANES)) for j in range(9)]
    return out


def ahead():
    return lax.shift_right_logical((64 - lax.axis_index("space")) * TILES, 6)


def pick(load, high, low):
    found = take(load(0), low)
    for tile in range(1, TILES):
        found = jnp.where(high == tile, take(load(tile), low), found)
    return found


def lists_body(up_ref, down_ref, nbr_ref, rows_ref, words_ref, codes_ref):
    at = lax.broadcasted_iota(I32, (8, LANES), 0) * LANES + lax.broadcasted_iota(I32, (8, LANES), 1)
    code = jnp.full((8, LANES), -1, I32)
    for j in range(8):
        code = jnp.where(at == up_ref[j], 8 + j, code)
        code = jnp.where(at == down_ref[j], j, code)
    codes_ref[...] = code
    lane = lax.broadcasted_iota(I32, (SLOTS, LANES), 1)
    bits = jnp.zeros((SLOTS, LANES), I32)
    for tile in range(TILES):
        block = nbr_ref[:, cols(tile)]
        empty = block == lane + tile * LANES
        rows_ref[tile] = jnp.where(empty, -1, block)
        mine = jnp.where(empty, 0, lax.shift_left(jnp.ones_like(block), lax.shift_right_logical(block, 7)))
        for step in (64, 32, 16, 8, 4, 2, 1):
            mine = mine | pltpu.roll(mine, step, axis=1)
        bits = jnp.where(lane == tile, mine, bits)
    word = jnp.where(bits != 0, 1 << 13, 0)
    previous = jnp.zeros_like(bits)
    for at in range(FAST):
        lowest = bits & -bits
        index = jnp.zeros_like(bits)
        for tile in range(1, 16):
            index = jnp.where(lowest == (1 << tile), tile, index)
        index = jnp.where(lowest == 0, previous, index)
        previous = index
        word = word | lax.shift_left(index, 4 * at)
        bits = bits & (bits - 1)
    words_ref[...] = word | jnp.where(bits != 0, 1 << 12, 0)


def kick_body(therm_hbm, noise_hbm, drift_hbm, noisem_hbm, q_ref, therm_ref, noise_ref, drift_ref, noisem_ref, sems, small):
    def copies(tile):
        at = cols(tile)
        return (
            pltpu.make_async_copy(therm_hbm.at[:, :, at], therm_ref.at[:, :, at], sems.at[0, tile]),
            pltpu.make_async_copy(noise_hbm.at[:, :, at], noise_ref.at[:, :, at], sems.at[1, tile]),
        )

    matrices = (
        pltpu.make_async_copy(drift_hbm, drift_ref, small.at[0]),
        pltpu.make_async_copy(noisem_hbm, noisem_ref, small.at[1]),
    )
    for copy in matrices:
        copy.start()
    for tile in range(TILES):
        for copy in copies(tile):
            copy.start()
    for copy in matrices:
        copy.wait()
    d0, n0 = drift_ref[0:HALF, :], noisem_ref[0:HALF, :]
    q_ref[0:HALF, ATOMS:ATOMS + LANES] = jnp.broadcast_to(d0[:, 0:1], (HALF, LANES))
    q_ref[HALF:48, ATOMS:ATOMS + LANES] = jnp.zeros((48 - HALF, LANES), F32)
    ncol = [[jnp.broadcast_to(n0[g * 8:g * 8 + 8, j:j + 1], (8, LANES)) for j in range(9)] for g in range(2)]
    diagonal = lax.broadcasted_iota(I32, (8, 9), 1) == lax.broadcasted_iota(I32, (8, 9), 0) + 1
    dcol = []
    for k in range(HALF):
        row = jnp.where(diagonal, jnp.broadcast_to(d0[k:k + 1, :], (8, 9)), 0.0)
        dcol.append(jnp.broadcast_to(jnp.sum(row, axis=1, keepdims=True), (8, LANES)))
    sub = lax.broadcasted_iota(I32, (8, LANES), 0)
    m4, m2, m1 = sub < 4, (sub & 2) == 0, (sub & 1) == 0

    def tile_step(tile, carry):
        at = cols(tile)
        for copy in copies(tile):
            copy.wait()
        for c in range(3):
            for g in range(2):
                v = [therm_ref[(g * 8 + k) * 3 + c, :, at] * dcol[g * 8 + k] for k in range(8)]
                for mask, step, count in ((m4, 4, 4), (m2, 2, 2), (m1, 1, 1)):
                    merged = []
                    for k in range(count):
                        a, b = v[k], v[k + count]
                        z = jnp.where(mask, b, a)
                        if step == 4:
                            moved = pltpu.roll(z, 4, axis=0)
                        else:
                            moved = jnp.where(mask, pltpu.roll(z, 8 - step, axis=0), pltpu.roll(z, step, axis=0))
                        merged.append(jnp.where(mask, a, b) + moved)
                    v = merged
                total = v[0]
                for j in range(9):
                    total = total + ncol[g][j] * noise_ref[(j * 3 + c) * 2 + g, :, at]
                q_ref[pl.ds(c * HALF + g * 8, 8), at] = total
        return carry

    lax.fori_loop(0, TILES, tile_step, 0)


def modes_body(up_ref, down_ref, pos_ref, mom_ref, ppos_ref, pmom_ref, const_ref, therm_ref, noise_ref, drift_ref,
               noisem_ref, modes_ref, part_ref, tcol, ncol):
    forward = const_ref[lax.axis_index("bead"), 0:BEADS, :]
    for c in range(3):
        r = slice(c * HALF, c * HALF + HALF)
        for at, (mine, other) in enumerate(((pos_ref, ppos_ref), (mom_ref, pmom_ref))):
            both = jnp.concatenate([mine[r, :], other[r, :]], axis=0)
            modes_ref[c, at] = jnp.dot(forward, both, precision=HIGHEST, preferred_element_type=F32)
    leave = leavers(up_ref, down_ref)
    high, low = lax.shift_right_logical(leave, 7), leave & 127

    def therm_step(g, carry):
        tcol[g] = pick(lambda t: therm_ref[g, :, cols(t)], high, low)
        return carry

    def noise_step(g, carry):
        ncol[g] = pick(lambda t: noise_ref[g, :, cols(t)], high, low)
        return carry

    lax.fori_loop(0, 48, therm_step, 0, unroll=12)
    lax.fori_loop(0, 54, noise_step, 0, unroll=18)
    for k in range(HALF):
        column = columns_of(drift_ref, noisem_ref, k)
        for c in range(3):
            total = None
            for j in range(8):
                term = column[1 + j] * spread(tcol[k * 3 + c, j:j + 1, :])
                total = term if total is None else total + term
            for j in range(9):
                total = total + column[9 + j] * spread(ncol[(j * 3 + c) * 2 + k // 8, k % 8:k % 8 + 1, :])
            part_ref[k * 3 + c] = total


def beads_body(up_ref, down_ref, modes_ref, q_ref, pq_ref, const_ref, part_ref, drift_ref, gup_ref, gdown_ref,
               pos_ref, mom_ref, mm_ref, ubuf_ref, dbuf_ref, upack_ref, dpack_ref, packs):
    core = lax.axis_index("bead")
    table = const_ref[core, 48:80, :]
    d00 = jnp.concatenate([q_ref[0:HALF, ATOMS:ATOMS + 1], pq_ref[0:HALF, ATOMS:ATOMS + 1]], axis=0)
    cosine, ratio, stiff = table[:, 0:1], table[:, 1:2], table[:, 2:3]
    backward = const_ref[core, 32:48, :]
    for c in range(3):
        r = slice(c * HALF, c * HALF + HALF)
        mode_pos, mode_mom = modes_ref[c, 0], modes_ref[c, 1]
        kicked = d00 * mode_mom + jnp.concatenate([q_ref[r, 0:ATOMS], pq_ref[r, 0:ATOMS]], axis=0)
        free_pos = cosine * mode_pos + ratio * kicked
        free_mom = cosine * kicked - stiff * mode_pos
        pos_ref[r, :] = jnp.dot(backward, free_pos, precision=HIGHEST, preferred_element_type=F32)
        mom_ref[r, :] = jnp.dot(backward, free_mom, precision=HIGHEST, preferred_element_type=F32)
        mm_ref[r, :] = mode_mom[0:HALF]

    for buf, ghost_ref in ((ubuf_ref, gup_ref), (dbuf_ref, gdown_ref)):
        for tile in range(GHOST_TILES):
            index = jnp.broadcast_to(ghost_ref[tile * LANES:tile * LANES + LANES].reshape(1, LANES), (8, LANES))
            high, low = lax.shift_right_logical(index, 7), index & 127
            for g in range(6):
                at = tile * 48 + g * 8
                buf[at:at + 8, :] = pick(lambda t: pos_ref[g * 8:g * 8 + 8, cols(t)], high, low)
            code = jnp.full((8, LANES), -1.0, F32)
            for j in range(8):
                code = jnp.where(index == up_ref[j], 8.0 + j, code)
                code = jnp.where(index == down_ref[j], 0.0 + j, code)
            buf[256 + tile:257 + tile, :] = code[0:1, :]
        buf[260:264, :] = jnp.zeros((4, LANES), F32)

    leave = leavers(up_ref, down_ref)
    high, low = lax.shift_right_logical(leave, 7), leave & 127
    group = lax.shift_right_logical(lax.broadcasted_iota(I32, (8, LANES), 1), 4)
    packed = [jnp.zeros((8, LANES), F32) for _ in range(8)]

    def put(at, value):
        packed[at // 8] = jnp.where(group == at % 8, value, packed[at // 8])

    for g in range(6):
        put(g, pick(lambda t: pos_ref[g * 8:g * 8 + 8, cols(t)], high, low))
        put(6 + g, pick(lambda t: mom_ref[g * 8:g * 8 + 8, cols(t)], high, low))
        packs[g] = pick(lambda t: mm_ref[g * 8:g * 8 + 8, cols(t)], high, low)
    for k in range(HALF):
        column = jnp.broadcast_to(drift_ref[pl.ds(HALF + k, 8, stride=HALF), 0:1], (8, LANES))
        for c in range(3):
            row = spread(packs[c * 2 + k // 8, k % 8:k % 8 + 1, :])
            put(12 + k * 3 + c, part_ref[k * 3 + c] + column * row)
    for buf in (ubuf_ref, dbuf_ref):
        for at in range(8):
            buf[192 + at * 8:200 + at * 8, :] = packed[at]
    upack_ref[...] = packed[0]
    dpack_ref[...] = packed[0]


def aux_work(first, last, therm_ref, noise_ref, mm_ref, drift_ref, noisem_ref, aux_ref):
    for k in range(HALF):
        column = columns_of(drift_ref, noisem_ref, k)

        def tile_step(tile, carry):
            at = cols(tile)
            for c in range(3):
                row = c * HALF + k
                total = column[0] * spread(mm_ref[row:row + 1, at])
                for j in range(8):
                    total = total + column[1 + j] * spread(therm_ref[k * 3 + c, j:j + 1, at])
                for j in range(9):
                    total = total + column[9 + j] * spread(noise_ref[(j * 3 + c) * 2 + k // 8, k % 8:k % 8 + 1, at])
                aux_ref[k * 3 + c, :, at] = total
            return carry

        lax.fori_loop(first, last, tile_step, 0)


def aux_first(therm_ref, noise_ref, mm_ref, drift_ref, noisem_ref, buf_in, pack_in, aux_ref, buf_out, pack_out):
    @pl.when(ahead() > 0)
    def _():
        aux_work(0, ahead(), therm_ref, noise_ref, mm_ref, drift_ref, noisem_ref, aux_ref)


def aux_second(therm_ref, noise_ref, mm_ref, drift_ref, noisem_ref, aux_ref):
    @pl.when(ahead() < TILES)
    def _():
        aux_work(ahead(), TILES, therm_ref, noise_ref, mm_ref, drift_ref, noisem_ref, aux_ref)


def force_body(words_vmem, codes, nbr_ref, pos_ref, mom_ref, aux_ref, aux2_ref, pack_ref, low_ref, high_ref,
               low2_ref, high2_ref, moved_hbm, momout_hbm, auxout_hbm, table, aux, moved_ref, momout_ref, words_ref,
               sems, tile_sems):
    fetch = pltpu.make_async_copy(words_vmem, words_ref, sems.at[0])
    fetch.start()
    lane = lax.broadcasted_iota(I32, (8, LANES), 1)
    from_low = (lane & 15) < 8
    packed = [
        jnp.where(from_low, low_ref[192 + at * 8:200 + at * 8, :], high_ref[192 + at * 8:200 + at * 8, :])
        for at in range(8)
    ]

    def own_tile(aux_from, tile, carry):
        at = cols(tile)
        mine = spread(codes[pl.ds(tile, 1), :])
        comes, base = mine >= 0, jnp.maximum(mine, 0)
        lanes = [base + 16 * m for m in range(8)]
        for g in range(6):
            r = slice(g * 8, g * 8 + 8)
            new = jnp.where(comes, take(packed[0], lanes[g]), pos_ref[r, at])
            table[tile, r, :] = new
            moved_ref[r, at] = new
            place = 6 + g
            momout_ref[r, at] = jnp.where(comes, take(packed[place // 8], lanes[place % 8]), mom_ref[r, at])
        for g in range(48):
            place = 12 + g
            aux[g, :, at] = jnp.where(comes, take(packed[place // 8], lanes[place % 8]), aux_from[g, :, at])
        return carry

    lax.fori_loop(0, ahead(), functools.partial(own_tile, aux_ref), 0)
    lax.fori_loop(ahead(), TILES, functools.partial(own_tile, aux2_ref), 0)
    outs = (
        pltpu.make_async_copy(moved_ref, moved_hbm, sems.at[1]),
        pltpu.make_async_copy(aux, auxout_hbm, sems.at[2]),
    )
    for out in outs:
        out.start()

    for side, (buf, source) in enumerate((
        (low_ref, jnp.where(from_low, low2_ref[...], pack_ref[...])),
        (high_ref, jnp.where(from_low, pack_ref[...], high2_ref[...])),
    )):
        for tile in range(GHOST_TILES):
            row = 256 + tile
            mine = spread(buf[row:row + 1, :]).astype(I32)
            comes, base = mine >= 0, jnp.maximum(mine, 0)
            for g in range(6):
                r = slice(g * 8, g * 8 + 8)
                old = buf[tile * 48 + g * 8:tile * 48 + g * 8 + 8, :]
                table[TILES + side * GHOST_TILES + tile, r, :] = jnp.where(comes, take(source, base + 16 * g), old)

    fetch.wait()

    def leave(tile):
        at = cols(tile)
        return pltpu.make_async_copy(momout_ref.at[:, at], momout_hbm.at[:, at], tile_sems.at[tile])

    def atom_tile(tile, carry):
        at = cols(tile)
        own = [table[tile, g * 8:g * 8 + 8, :] for g in range(6)]

        def pull(found, high, low, place):
            hit = high == place
            return [jnp.where(hit, take(table[place, g * 8:g * 8 + 8, :], low), found[g]) for g in range(6)]

        def push(total, found):
            done = list(total)
            for half in range(2):
                d = [own[2 * c + half] - found[2 * c + half] for c in range(3)]
                weight = jnp.exp((d[0] * d[0] + d[1] * d[1] + d[2] * d[2]) * (-0.5 / core_width))
                for c in range(3):
                    done[2 * c + half] = done[2 * c + half] + d[c] * weight
            return tuple(done)

        def chunk(number, total):
            first = number * CHUNK
            words = [words_ref[first + u, tile] for u in range(CHUNK)]
            seen = words[0]
            for word in words[1:]:
                seen = seen | word

            def index_of(u):
                index = spread(nbr_ref[tile, pl.ds(first + u, 1), :])
                return index, lax.shift_right_arithmetic(index, 7), index & 127

            def fast(total):
                for u in range(CHUNK):
                    _, high, low = index_of(u)
                    found = own
                    for at_most in range(FAST):
                        place = lax.shift_right_logical(words[u], 4 * at_most) & 15
                        found = pull(found, high, low, place)
                    total = push(total, found)
                return total

            def slow(total):
                def one(u, total):
                    _, high, low = index_of(u)
                    found = lax.fori_loop(0, 16, lambda place, found: tuple(pull(found, high, low, place)), tuple(own))
                    return push(total, found)

                return lax.fori_loop(0, CHUNK, one, total)

            def some(total):
                return lax.cond((seen & (1 << 12)) != 0, slow, fast, total)

            return lax.cond((seen & (1 << 13)) != 0, some, lambda total: total, total)

        zero = jnp.zeros((8, LANES), F32)
        total = lax.fori_loop(0, SLOTS // CHUNK, chunk, (zero,) * 6)
        for g in range(6):
            r = slice(g * 8, g * 8 + 8)
            momout_ref[r, at] = momout_ref[r, at] + kick_scale * total[g]
        leave(tile).start()
        return carry

    lax.fori_loop(0, TILES, atom_tile, 0)
    for out in outs:
        out.wait()
    for tile in range(TILES):
        leave(tile).wait()


def per_device(positions, momenta, thermostat, white_noise, drift_matrix, noise_matrix, leave_up, leave_down,
               ghost_up, ghost_down, neighbours):
    pos = positions.transpose(1, 0, 2).reshape(48, ATOMS)
    mom = momenta.transpose(1, 0, 2).reshape(48, ATOMS)
    therm = thermostat.transpose(0, 2, 1, 3).reshape(48, 8, ATOMS)
    noise = white_noise.transpose(1, 2, 0, 3).reshape(54, 8, ATOMS)
    drift = drift_matrix.transpose(1, 0, 2).reshape(144, 9)
    noisem = noise_matrix.transpose(1, 0, 2).reshape(144, 9)
    const = jnp.asarray(CONSTANTS)

    other_pos = shifted(pos, "bead", 1)
    other_mom = shifted(mom, "bead", 1)
    held = [pltpu.with_memory_space_constraint(x, pltpu.HBM) for x in (therm, noise, drift, noisem)]
    q, therm, noise, drift, noisem = call(
        kick_body,
        [struct(48, ATOMS + LANES), struct(48, 8, ATOMS), struct(54, 8, ATOMS), struct(144, 9), struct(144, 9)],
        held, specs=[HBM] * 4,
        scratch=[pltpu.SemaphoreType.DMA((2, TILES)), pltpu.SemaphoreType.DMA((2,))], flops=4000000, nbytes=3600000,
    )
    other_q = shifted(q, "bead", 1)
    modes, part = call(
        modes_body,
        [struct(3, 2, BEADS, ATOMS), struct(48, 8, LANES)],
        [leave_up, leave_down, pos, mom, other_pos, other_mom, const, therm, noise, drift, noisem],
        specs=[SMEM] * 2 + [VMEM] * 9,
        scratch=[pltpu.VMEM((48, 8, LANES), F32), pltpu.VMEM((54, 8, LANES), F32)],
        flops=8000000, nbytes=4000000,
    )
    bead_pos, bead_mom, mode_mom, up_buf, down_buf, up_pack, down_pack = call(
        beads_body,
        [struct(48, ATOMS)] * 3 + [struct(264, LANES)] * 2 + [struct(8, LANES)] * 2,
        [leave_up, leave_down, modes, q, other_q, const, part, drift, ghost_up, ghost_down],
        specs=[SMEM] * 2 + [VMEM] * 8,
        scratch=[pltpu.VMEM((6, 8, LANES), F32)],
        flops=8000000, nbytes=2000000,
    )
    low = shifted(up_buf, "space", 1)
    low2 = shifted(up_pack, "space", 2)
    work = [therm, noise, mode_mom, drift, noisem]
    aux, down_buf, down_pack = call(
        aux_first, [struct(48, 8, ATOMS), struct(264, LANES), struct(8, LANES)], work + [down_buf, down_pack],
        specs=[VMEM] * 5 + [ANY] * 2, out_specs=[VMEM, ANY, ANY], alias={5: 1, 6: 2}, flops=1000, nbytes=1000,
    )
    high = shifted(down_buf, "space", -1)
    high2 = shifted(down_pack, "space", -2)
    (aux2,) = call(aux_second, [struct(48, 8, ATOMS)], work, flops=16000000, nbytes=5000000)
    rows, words, codes = call(
        lists_body,
        [struct(TILES, SLOTS, LANES, dtype=I32), struct(SLOTS, LANES, dtype=I32), struct(8, LANES, dtype=I32)],
        [leave_up, leave_down, neighbours], specs=[SMEM, SMEM, VMEM],
        flops=1000000, nbytes=300000,
    )
    moved, slab, out_aux = call(
        force_body,
        [struct(48, ATOMS), struct(48, ATOMS), struct(48, 8, ATOMS)],
        [words, codes, rows, bead_pos, bead_mom, aux, aux2, up_pack, low, high, low2, high2],
        out_specs=[HBM] * 3,
        scratch=[
            pltpu.VMEM((2 * TILES, 48, LANES), F32),
            pltpu.VMEM((48, 8, ATOMS), F32),
            pltpu.VMEM((48, ATOMS), F32),
            pltpu.VMEM((48, ATOMS), F32),
            pltpu.SMEM((SLOTS, LANES), I32),
            pltpu.SemaphoreType.DMA((3,)),
            pltpu.SemaphoreType.DMA((TILES,)),
        ],
        flops=30000000, nbytes=4000000,
    )
    moved = moved.reshape(3, HALF, ATOMS).transpose(1, 0, 2)
    slab = slab.reshape(3, HALF, ATOMS).transpose(1, 0, 2)
    out_aux = out_aux.reshape(HALF, 3, 8, ATOMS).transpose(0, 2, 1, 3)
    return (moved, slab, out_aux)


def solution(mesh):
    in_specs = (
        P("bead", None, "space"),
        P("bead", None, "space"),
        P("bead", None, None, "space"),
        P("bead", None, None, "space"),
        P("bead", None, None),
        P("bead", None, None),
        P("space"),
        P("space"),
        P("space"),
        P("space"),
        P(None, "space"),
    )
    out_specs = (P("bead", None, "space"), P("bead", None, "space"), P("bead", None, None, "space"))

    return jax.shard_map(per_device, mesh=mesh, in_specs=in_specs, out_specs=out_specs, check_vma=False)
```

```python
import math

import jax
import jax.numpy as jnp
import numpy as np
from jax import lax
from jax.experimental import pallas as pl
from jax.experimental.pallas import tpu as pltpu
from jax.sharding import PartitionSpec as P


BEADS = 32
HALF = 16
ATOMS = 1024
TILES = 8
SLOTS = 32
GHOST_TILES = 4
LANES = 128
WINDOWS = 32
EMPTY = 4095
CHUNK = 32

cycle_rate = 0.8
kick_scale = 0.2
core_width = 4.0

F32 = jnp.float32
I32 = jnp.int32
VMEM = pl.BlockSpec(memory_space=pltpu.VMEM)
SMEM = pl.BlockSpec(memory_space=pltpu.SMEM)
ANY = pl.BlockSpec(memory_space=pl.ANY)
HBM = pl.BlockSpec(memory_space=pltpu.HBM)


def constants():
    k = np.arange(BEADS)[:, None].astype(np.float64)
    b = np.arange(BEADS)[None, :].astype(np.float64)
    angle = 2.0 * math.pi * ((k * b) % BEADS) / BEADS
    scale = math.sqrt(2.0 / BEADS)
    basis = np.where(k < BEADS // 2, scale * np.cos(angle), scale * np.sin(angle))
    basis = np.where(k == 0, 1.0 / math.sqrt(BEADS), basis)
    basis = np.where(k == BEADS // 2, np.cos(math.pi * b) / math.sqrt(BEADS), basis)
    w = 2.0 * cycle_rate * np.sin(math.pi * np.arange(BEADS) / BEADS)
    ratio = np.where(w > 0, np.sin(w) / np.where(w > 0, w, 1.0), 1.0)
    columns = np.stack([np.cos(w), ratio, w * np.sin(w)], axis=1)

    def stacked(matrix):
        high = matrix.astype(jnp.bfloat16)
        low = (matrix - high.astype(np.float64)).astype(jnp.bfloat16)
        return np.concatenate([high, high, low], axis=1)

    matrices, tables = [], []
    for core in range(2):
        order = np.roll(np.arange(BEADS), -HALF * core)
        forward = basis[order][:, order]
        matrices.append(stacked(np.concatenate([forward, forward.T[:HALF]], axis=0)))
        tables.append(np.pad(columns[order], ((0, 0), (0, 5))))
    return np.stack(matrices), np.stack(tables).astype(np.float32)


MATRICES, TABLES = constants()


def call(body, outs, args, specs=None, out_specs=None, scratch=(), flops=0, nbytes=0, limit=24, alias=None):
    return pl.pallas_call(
        body,
        out_shape=outs,
        in_specs=specs or [VMEM] * len(args),
        out_specs=out_specs or [VMEM] * len(outs),
        scratch_shapes=scratch,
        input_output_aliases=alias or {},
        compiler_params=pltpu.CompilerParams(vmem_limit_bytes=limit << 20),
        cost_estimate=pl.CostEstimate(flops=flops, bytes_accessed=nbytes, transcendentals=0),
    )(*args)


def struct(*shape, dtype=F32):
    return jax.ShapeDtypeStruct(shape, dtype)


def shifted(array, axis, by):
    devices = lax.axis_size(axis)
    return lax.ppermute(array, axis, [(i, (i + by) % devices) for i in range(devices)])


def take(values, lanes):
    return lax.gather(
        values,
        lanes[..., None],
        lax.GatherDimensionNumbers(
            offset_dims=(),
            collapsed_slice_dims=(1,),
            start_index_map=(1,),
            operand_batching_dims=(0,),
            start_indices_batching_dims=(0,),
        ),
        slice_sizes=(1, 1),
        mode=lax.GatherScatterMode.PROMISE_IN_BOUNDS,
    )


def transform(matrix, values):
    high = values.astype(jnp.bfloat16)
    low = (values - high.astype(F32)).astype(jnp.bfloat16)
    return jnp.dot(matrix, jnp.concatenate([high, low, high], axis=0), preferred_element_type=F32)


def spread(row):
    return jnp.broadcast_to(row, (8, LANES))


def cols(tile):
    if isinstance(tile, int):
        return pl.ds(tile * LANES, LANES)
    return pl.ds(pl.multiple_of(tile * LANES, LANES), LANES)


def leavers(up_ref, down_ref):
    place = lax.broadcasted_iota(I32, (8, LANES), 1) & 15
    index = jnp.zeros((8, LANES), I32)
    for j in range(8):
        index = jnp.where(place == j, up_ref[j], index)
        index = jnp.where(place == 8 + j, down_ref[j], index)
    return index


def ahead():
    slab = lax.axis_index("space")
    way = 3 * (slab & 3) + 3 * (lax.shift_right_logical(slab, 2) & 3) + 5 * lax.shift_right_logical(slab, 4)
    return TILES - lax.shift_right_logical(way * TILES + HALF, 5)


def pick(load, high, low):
    found = take(load(0), low)
    for tile in range(1, TILES):
        found = jnp.where(high == tile, take(load(tile), low), found)
    return found


def make_lists(nbr_ref, rows_ref, words_ref):
    lane = lax.broadcasted_iota(I32, (SLOTS, LANES), 1)
    masks = []
    for tile in range(TILES):
        block = nbr_ref[:, cols(tile)]
        mine = lax.shift_left(jnp.ones_like(block), lax.shift_right_logical(block, 6))
        masks.append(jnp.where(block == lane + tile * LANES, 0, mine))
    for step, count in ((64, 4), (32, 2), (16, 1)):
        lower = (lane & step) == 0
        merged = []
        for at in range(count):
            first, second = masks[at], masks[at + count]
            other = jnp.where(lower, second, first)
            moved = jnp.where(lower, pltpu.roll(other, LANES - step, axis=1), pltpu.roll(other, step, axis=1))
            merged.append(jnp.where(lower, first, second) | moved)
        masks = merged
    bits = masks[0]
    for step in (8, 4, 2, 1):
        bits = bits | pltpu.roll(bits, LANES - step, axis=1)
    window = jnp.zeros_like(bits)
    wide = jnp.ones_like(bits)
    for at in range(WINDOWS):
        covered = sum(1 << ((at + i) % WINDOWS) for i in range(4))
        covered = covered - (1 << 32) if covered >= 1 << 31 else covered
        fits = (bits & ~covered) == 0
        window = jnp.where(fits, at, window)
        wide = jnp.where(fits, 0, wide)
    words_ref[...] = window | (wide << 8) | jnp.where(bits != 0, 1 << 9, 0)
    for tile in range(TILES):
        block = nbr_ref[:, cols(tile)]
        start = jnp.broadcast_to(window[:, 16 * tile:16 * tile + 1], (SLOTS, LANES)) << 6
        rows_ref[tile] = jnp.where(block == lane + tile * LANES, EMPTY, (block - start) & 2047)


def kick_body(therm_hbm, noise_hbm, drift_hbm, noisem_hbm, nbr_hbm, q_ref, therm_ref, noise_ref, coef_ref, rows_ref,
              words_ref, drift_ref, noisem_ref, nbr_ref, sems, small):
    def copies(tile):
        at = cols(tile)
        return (
            pltpu.make_async_copy(therm_hbm.at[:, :, at], therm_ref.at[:, :, at], sems.at[0, tile]),
            pltpu.make_async_copy(noise_hbm.at[:, :, at], noise_ref.at[:, :, at], sems.at[1, tile]),
        )

    matrices = (
        pltpu.make_async_copy(drift_hbm, drift_ref, small.at[0]),
        pltpu.make_async_copy(noisem_hbm, noisem_ref, small.at[1]),
        pltpu.make_async_copy(nbr_hbm, nbr_ref, small.at[2]),
    )
    for copy in matrices:
        copy.start()

    def begin(tile, carry):
        for copy in copies(tile):
            copy.start()
        return carry

    lax.fori_loop(0, TILES, begin, 0)
    for copy in matrices:
        copy.wait()
    make_lists(nbr_ref, rows_ref, words_ref)
    for k in range(HALF):
        for at, ref in enumerate((drift_ref, noisem_ref)):
            block = ref[pl.ds(HALF + k, 8, stride=HALF), :]
            for j in range(9):
                coef_ref[k * 18 + at * 9 + j] = jnp.broadcast_to(block[:, j:j + 1], (8, LANES))
    d0, n0 = drift_ref[0:HALF, :], noisem_ref[0:HALF, :]
    q_ref[0:HALF, ATOMS:ATOMS + LANES] = jnp.broadcast_to(d0[:, 0:1], (HALF, LANES))
    q_ref[HALF:48, ATOMS:ATOMS + LANES] = jnp.zeros((48 - HALF, LANES), F32)
    ncol = [[jnp.broadcast_to(n0[g * 8:g * 8 + 8, j:j + 1], (8, LANES)) for j in range(9)] for g in range(2)]
    diagonal = lax.broadcasted_iota(I32, (8, 9), 1) == lax.broadcasted_iota(I32, (8, 9), 0) + 1
    dcol = []
    for k in range(HALF):
        row = jnp.where(diagonal, jnp.broadcast_to(d0[k:k + 1, :], (8, 9)), 0.0)
        dcol.append(jnp.broadcast_to(jnp.sum(row, axis=1, keepdims=True), (8, LANES)))
    sub = lax.broadcasted_iota(I32, (8, LANES), 0)
    m4, m2, m1 = sub < 4, (sub & 2) == 0, (sub & 1) == 0

    def tile_step(tile, carry):
        at = cols(tile)
        for copy in copies(tile):
            copy.wait()
        for c in range(3):
            for g in range(2):
                v = [therm_ref[(g * 8 + k) * 3 + c, :, at] * dcol[g * 8 + k] for k in range(8)]
                for mask, step, count in ((m4, 4, 4), (m2, 2, 2), (m1, 1, 1)):
                    merged = []
                    for k in range(count):
                        a, b = v[k], v[k + count]
                        z = jnp.where(mask, b, a)
                        if step == 4:
                            moved = pltpu.roll(z, 4, axis=0)
                        else:
                            moved = jnp.where(mask, pltpu.roll(z, 8 - step, axis=0), pltpu.roll(z, step, axis=0))
                        merged.append(jnp.where(mask, a, b) + moved)
                    v = merged
                total = v[0]
                for j in range(9):
                    total = total + ncol[g][j] * noise_ref[(j * 3 + c) * 2 + g, :, at]
                q_ref[pl.ds(c * HALF + g * 8, 8), at] = total
        return carry

    lax.fori_loop(0, TILES, tile_step, 0)


def modes_body(up_ref, down_ref, pos_ref, mom_ref, ppos_ref, pmom_ref, const_ref, therm_ref, noise_ref, coef_ref,
               modes_ref, part_ref, tcol, ncol):
    forward = const_ref[lax.axis_index("bead"), 0:BEADS, :]
    for c in range(3):
        r = slice(c * HALF, c * HALF + HALF)
        for at, (mine, other) in enumerate(((pos_ref, ppos_ref), (mom_ref, pmom_ref))):
            modes_ref[c, at] = transform(forward, jnp.concatenate([mine[r, :], other[r, :]], axis=0))
    leave = leavers(up_ref, down_ref)
    high, low = lax.shift_right_logical(leave, 7), leave & 127

    def therm_step(g, carry):
        tcol[g] = pick(lambda t: therm_ref[g, :, cols(t)], high, low)
        return carry

    def noise_step(g, carry):
        ncol[g] = pick(lambda t: noise_ref[g, :, cols(t)], high, low)
        return carry

    lax.fori_loop(0, 48, therm_step, 0, unroll=12)
    lax.fori_loop(0, 54, noise_step, 0, unroll=18)
    for k in range(HALF):
        for c in range(3):
            total = None
            for j in range(8):
                term = coef_ref[k * 18 + 1 + j] * spread(tcol[k * 3 + c, j:j + 1, :])
                total = term if total is None else total + term
            for j in range(9):
                row = spread(ncol[(j * 3 + c) * 2 + k // 8, k % 8:k % 8 + 1, :])
                total = total + coef_ref[k * 18 + 9 + j] * row
            part_ref[k * 3 + c] = total


def beads_body(up_ref, down_ref, modes_ref, q_ref, pq_ref, const_ref, table_ref, part_ref, coef_ref, gup_ref, gdown_ref,
               pos_ref, mom_ref, mm_ref, ubuf_ref, dbuf_ref, upack_ref, dpack_ref, codes_ref, packs):
    core = lax.axis_index("bead")
    table = table_ref[core]
    d00 = jnp.concatenate([q_ref[0:HALF, ATOMS:ATOMS + 1], pq_ref[0:HALF, ATOMS:ATOMS + 1]], axis=0)
    cosine, ratio, stiff = table[:, 0:1], table[:, 1:2], table[:, 2:3]
    backward = const_ref[core, 32:48, :]
    for c in range(3):
        r = slice(c * HALF, c * HALF + HALF)
        mode_pos, mode_mom = modes_ref[c, 0], modes_ref[c, 1]
        kicked = d00 * mode_mom + jnp.concatenate([q_ref[r, 0:ATOMS], pq_ref[r, 0:ATOMS]], axis=0)
        free_pos = cosine * mode_pos + ratio * kicked
        free_mom = cosine * kicked - stiff * mode_pos
        pos_ref[r, :] = transform(backward, free_pos)
        mom_ref[r, :] = transform(backward, free_mom)
        mm_ref[r, :] = mode_mom[0:HALF]

    for buf, ghost_ref in ((ubuf_ref, gup_ref), (dbuf_ref, gdown_ref)):
        for tile in range(GHOST_TILES):
            index = jnp.broadcast_to(ghost_ref[tile * LANES:tile * LANES + LANES].reshape(1, LANES), (8, LANES))
            high, low = lax.shift_right_logical(index, 7), index & 127
            for g in range(6):
                at = tile * 48 + g * 8
                buf[at:at + 8, :] = pick(lambda t: pos_ref[g * 8:g * 8 + 8, cols(t)], high, low)
            code = jnp.full((8, LANES), -1.0, F32)
            for j in range(8):
                code = jnp.where(index == up_ref[j], 8.0 + j, code)
                code = jnp.where(index == down_ref[j], 0.0 + j, code)
            buf[256 + tile:257 + tile, :] = code[0:1, :]
        buf[260:264, :] = jnp.zeros((4, LANES), F32)

    leave = leavers(up_ref, down_ref)
    high, low = lax.shift_right_logical(leave, 7), leave & 127
    group = lax.shift_right_logical(lax.broadcasted_iota(I32, (8, LANES), 1), 4)
    packed = [jnp.zeros((8, LANES), F32) for _ in range(8)]

    def put(at, value):
        packed[at // 8] = jnp.where(group == at % 8, value, packed[at // 8])

    for g in range(6):
        put(g, pick(lambda t: pos_ref[g * 8:g * 8 + 8, cols(t)], high, low))
        put(6 + g, pick(lambda t: mom_ref[g * 8:g * 8 + 8, cols(t)], high, low))
        packs[g] = pick(lambda t: mm_ref[g * 8:g * 8 + 8, cols(t)], high, low)
    for k in range(HALF):
        column = coef_ref[k * 18]
        for c in range(3):
            row = spread(packs[c * 2 + k // 8, k % 8:k % 8 + 1, :])
            put(12 + k * 3 + c, part_ref[k * 3 + c] + column * row)
    for buf in (ubuf_ref, dbuf_ref):
        for at in range(8):
            buf[192 + at * 8:200 + at * 8, :] = packed[at]
    upack_ref[...] = packed[0]
    dpack_ref[...] = packed[0]
    at = lax.broadcasted_iota(I32, (8, LANES), 0) * LANES + lax.broadcasted_iota(I32, (8, LANES), 1)
    code = jnp.full((8, LANES), -1, I32)
    for j in range(8):
        code = jnp.where(at == up_ref[j], 8 + j, code)
        code = jnp.where(at == down_ref[j], j, code)
    codes_ref[...] = code


def aux_work(first, last, therm_ref, noise_ref, mm_ref, coef_ref, aux_ref):
    def tile_step(tile, carry):
        at = cols(tile)
        for k in range(HALF):
            column = [coef_ref[k * 18 + j] for j in range(18)]
            for c in range(3):
                row = c * HALF + k
                total = column[0] * spread(mm_ref[row:row + 1, at])
                for j in range(8):
                    total = total + column[1 + j] * spread(therm_ref[k * 3 + c, j:j + 1, at])
                for j in range(9):
                    total = total + column[9 + j] * spread(noise_ref[(j * 3 + c) * 2 + k // 8, k % 8:k % 8 + 1, at])
                aux_ref[k * 3 + c, :, at] = total
        return carry

    lax.fori_loop(first, last, tile_step, 0)


def aux_first(therm_ref, noise_ref, mm_ref, coef_ref, buf_in, pack_in, aux_ref, buf_out, pack_out):
    aux_work(0, ahead(), therm_ref, noise_ref, mm_ref, coef_ref, aux_ref)


def aux_second(done_ref, therm_ref, noise_ref, mm_ref, coef_ref, aux_ref):
    aux_work(ahead(), TILES, therm_ref, noise_ref, mm_ref, coef_ref, aux_ref)


def force_body(words_vmem, codes, nbr_ref, pos_ref, mom_ref, aux_ref, pack_ref, low_ref, high_ref,
               low2_ref, high2_ref, moved_hbm, momout_hbm, auxout_hbm, table, aux, moved_ref, momout_ref, words_ref,
               sems, tile_sems):
    fetch = pltpu.make_async_copy(words_vmem, words_ref, sems.at[0])
    fetch.start()
    lane = lax.broadcasted_iota(I32, (8, LANES), 1)
    from_low = (lane & 15) < 8
    packed = [
        jnp.where(from_low, low_ref[192 + at * 8:200 + at * 8, :], high_ref[192 + at * 8:200 + at * 8, :])
        for at in range(8)
    ]

    def own_tile(tile, carry):
        at = cols(tile)
        mine = spread(codes[pl.ds(tile, 1), :])
        comes, base = mine >= 0, jnp.maximum(mine, 0)
        lanes = [base + 16 * m for m in range(8)]
        for g in range(6):
            r = slice(g * 8, g * 8 + 8)
            new = jnp.where(comes, take(packed[0], lanes[g]), pos_ref[r, at])
            table[2 * tile, r, :] = new
            moved_ref[r, at] = new
            place = 6 + g
            momout_ref[r, at] = jnp.where(comes, take(packed[place // 8], lanes[place % 8]), mom_ref[r, at])
        for g in range(48):
            place = 12 + g
            aux[g, :, at] = jnp.where(comes, take(packed[place // 8], lanes[place % 8]), aux_ref[g, :, at])
        return carry

    lax.fori_loop(0, TILES, own_tile, 0, unroll=2)
    outs = (
        pltpu.make_async_copy(moved_ref, moved_hbm, sems.at[1]),
        pltpu.make_async_copy(aux, auxout_hbm, sems.at[2]),
    )
    for out in outs:
        out.start()

    for side, (buf, source) in enumerate((
        (low_ref, jnp.where(from_low, low2_ref[...], pack_ref[...])),
        (high_ref, jnp.where(from_low, pack_ref[...], high2_ref[...])),
    )):
        for tile in range(GHOST_TILES):
            row = 256 + tile
            mine = spread(buf[row:row + 1, :]).astype(I32)
            comes, base = mine >= 0, jnp.maximum(mine, 0)
            for g in range(6):
                r = slice(g * 8, g * 8 + 8)
                old = buf[tile * 48 + g * 8:tile * 48 + g * 8 + 8, :]
                table[2 * (TILES + side * GHOST_TILES + tile), r, :] = jnp.where(comes, take(source, base + 16 * g), old)

    for g in range(6):
        r = slice(g * 8, g * 8 + 8)
        rolled = [pltpu.roll(table[2 * tile, r, :], 64, axis=1) for tile in range(2 * TILES)]
        for tile in range(2 * TILES):
            table[2 * tile + 1, r, :] = jnp.where(lane < 64, rolled[tile], rolled[(tile + 1) % (2 * TILES)])
    fetch.wait()

    def leave(tile):
        at = cols(tile)
        return pltpu.make_async_copy(momout_ref.at[:, at], momout_hbm.at[:, at], tile_sems.at[tile])

    def atom_tile(tile, carry):
        at = cols(tile)
        own = [table[2 * tile, g * 8:g * 8 + 8, :] for g in range(6)]

        def pull(found, hit, low, place):
            return [jnp.where(hit, take(table[place, g * 8:g * 8 + 8, :], low), found[g]) for g in range(6)]

        def push(total, found):
            done = list(total)
            for half in range(2):
                d = [own[2 * c + half] - found[2 * c + half] for c in range(3)]
                weight = jnp.exp((d[0] * d[0] + d[1] * d[1] + d[2] * d[2]) * (-0.5 / core_width))
                for c in range(3):
                    done[2 * c + half] = done[2 * c + half] + d[c] * weight
            return tuple(done)

        def chunk(number, total):
            first = number * CHUNK
            words = [words_ref[first + u, 16 * tile] for u in range(CHUNK)]
            seen = words[0]
            for word in words[1:]:
                seen = seen | word

            def fast(total):
                for u in range(CHUNK):
                    index = spread(nbr_ref[tile, pl.ds(first + u, 1), :])
                    high, low = lax.shift_right_logical(index, 7), index & 127
                    place = words[u] & 31
                    found = pull(own, high == 0, low, place)
                    total = push(total, pull(found, high == 1, low, (place + 2) & 31))
                return total

            def slow(total):
                def one(u, total):
                    index = spread(nbr_ref[tile, pl.ds(first + u, 1), :])
                    index = jnp.where(index == EMPTY, EMPTY, (index + (words_ref[first + u, 16 * tile] & 31) * 64) & 2047)
                    high, low = lax.shift_right_logical(index, 7), index & 127
                    found = lax.fori_loop(
                        0, 16, lambda place, found: tuple(pull(found, high == place, low, 2 * place)), tuple(own)
                    )
                    return push(total, found)

                return lax.fori_loop(0, CHUNK, one, total)

            def some(total):
                return lax.cond((seen & (1 << 8)) != 0, slow, fast, total)

            return lax.cond((seen & (1 << 9)) != 0, some, lambda total: total, total)

        zero = jnp.zeros((8, LANES), F32)
        total = lax.fori_loop(0, SLOTS // CHUNK, chunk, (zero,) * 6)
        for g in range(6):
            r = slice(g * 8, g * 8 + 8)
            momout_ref[r, at] = momout_ref[r, at] + kick_scale * total[g]
        leave(tile).start()
        return carry

    lax.fori_loop(0, TILES, atom_tile, 0)
    for out in outs:
        out.wait()
    for tile in range(TILES):
        leave(tile).wait()


def per_device(positions, momenta, thermostat, white_noise, drift_matrix, noise_matrix, leave_up, leave_down,
               ghost_up, ghost_down, neighbours):
    pos = positions.transpose(1, 0, 2).reshape(48, ATOMS)
    mom = momenta.transpose(1, 0, 2).reshape(48, ATOMS)
    therm = thermostat.transpose(0, 2, 1, 3).reshape(48, 8, ATOMS)
    noise = white_noise.transpose(1, 2, 0, 3).reshape(54, 8, ATOMS)
    drift = drift_matrix.transpose(1, 0, 2).reshape(144, 9)
    noisem = noise_matrix.transpose(1, 0, 2).reshape(144, 9)
    matrices, tables = jnp.asarray(MATRICES), jnp.asarray(TABLES)

    other_pos = shifted(pos, "bead", 1)
    other_mom = shifted(mom, "bead", 1)
    held = [pltpu.with_memory_space_constraint(x, pltpu.HBM) for x in (therm, noise, drift, noisem, neighbours)]
    q, therm, noise, coef, rows, words = call(
        kick_body,
        [
            struct(48, ATOMS + LANES), struct(48, 8, ATOMS), struct(54, 8, ATOMS), struct(288, 8, LANES),
            struct(TILES, SLOTS, LANES, dtype=I32), struct(SLOTS, LANES, dtype=I32),
        ],
        held, specs=[HBM] * 5,
        scratch=[
            pltpu.VMEM((144, 9), F32), pltpu.VMEM((144, 9), F32), pltpu.VMEM((SLOTS, ATOMS), I32),
            pltpu.SemaphoreType.DMA((2, TILES)), pltpu.SemaphoreType.DMA((3,)),
        ],
        flops=4000000, nbytes=3600000,
    )
    other_q = shifted(q, "bead", 1)
    modes, part = call(
        modes_body,
        [struct(3, 2, BEADS, ATOMS), struct(48, 8, LANES)],
        [leave_up, leave_down, pos, mom, other_pos, other_mom, matrices, therm, noise, coef],
        specs=[SMEM] * 2 + [VMEM] * 8,
        scratch=[pltpu.VMEM((48, 8, LANES), F32), pltpu.VMEM((54, 8, LANES), F32)],
        flops=8000000, nbytes=4000000,
    )
    bead_pos, bead_mom, mode_mom, up_buf, down_buf, up_pack, down_pack, codes = call(
        beads_body,
        [struct(48, ATOMS)] * 3 + [struct(264, LANES)] * 2 + [struct(8, LANES)] * 2 + [struct(8, LANES, dtype=I32)],
        [leave_up, leave_down, modes, q, other_q, matrices, tables, part, coef, ghost_up, ghost_down],
        specs=[SMEM] * 2 + [VMEM] * 9,
        scratch=[pltpu.VMEM((6, 8, LANES), F32)],
        flops=8000000, nbytes=2000000,
    )
    low = shifted(up_buf, "space", 1)
    low2 = shifted(up_pack, "space", 2)
    work = [therm, noise, mode_mom, coef]
    aux, down_buf, down_pack = call(
        aux_first, [struct(48, 8, ATOMS), struct(264, LANES), struct(8, LANES)], work + [down_buf, down_pack],
        specs=[VMEM] * 4 + [ANY] * 2, out_specs=[VMEM, ANY, ANY], alias={4: 1, 5: 2}, flops=1000, nbytes=1000,
    )
    high = shifted(down_buf, "space", -1)
    high2 = shifted(down_pack, "space", -2)
    (aux,) = call(aux_second, [struct(48, 8, ATOMS)], [aux] + work, alias={0: 0}, flops=16000000, nbytes=5000000)
    moved, slab, out_aux = call(
        force_body,
        [struct(48, ATOMS), struct(48, ATOMS), struct(48, 8, ATOMS)],
        [words, codes, rows, bead_pos, bead_mom, aux, up_pack, low, high, low2, high2],
        out_specs=[HBM] * 3,
        scratch=[
            pltpu.VMEM((WINDOWS, 48, LANES), F32),
            pltpu.VMEM((48, 8, ATOMS), F32),
            pltpu.VMEM((48, ATOMS), F32),
            pltpu.VMEM((48, ATOMS), F32),
            pltpu.SMEM((SLOTS, LANES), I32),
            pltpu.SemaphoreType.DMA((3,)),
            pltpu.SemaphoreType.DMA((TILES,)),
        ],
        flops=30000000, nbytes=4000000,
    )
    moved = moved.reshape(3, HALF, ATOMS).transpose(1, 0, 2)
    slab = slab.reshape(3, HALF, ATOMS).transpose(1, 0, 2)
    out_aux = out_aux.reshape(HALF, 3, 8, ATOMS).transpose(0, 2, 1, 3)
    return (moved, slab, out_aux)


def solution(mesh):
    in_specs = (
        P("bead", None, "space"),
        P("bead", None, "space"),
        P("bead", None, None, "space"),
        P("bead", None, None, "space"),
        P("bead", None, None),
        P("bead", None, None),
        P("space"),
        P("space"),
        P("space"),
        P("space"),
        P(None, "space"),
    )
    out_specs = (P("bead", None, "space"), P("bead", None, "space"), P("bead", None, None, "space"))

    return jax.shard_map(per_device, mesh=mesh, in_specs=in_specs, out_specs=out_specs, check_vma=False)
```

```python
import math

import jax
import jax.numpy as jnp
import numpy as np
from jax import lax
from jax.experimental import pallas as pl
from jax.experimental.pallas import tpu as pltpu
from jax.sharding import PartitionSpec as P


BEADS = 32
HALF = 16
ATOMS = 1024
TILES = 8
SLOTS = 32
GHOST_TILES = 4
LANES = 128
WINDOWS = 32
EMPTY = 4095
CHUNK = 32

cycle_rate = 0.8
kick_scale = 0.2
core_width = 4.0

F32 = jnp.float32
I32 = jnp.int32
VMEM = pl.BlockSpec(memory_space=pltpu.VMEM)
SMEM = pl.BlockSpec(memory_space=pltpu.SMEM)
ANY = pl.BlockSpec(memory_space=pl.ANY)
HBM = pl.BlockSpec(memory_space=pltpu.HBM)


def constants():
    k = np.arange(BEADS)[:, None].astype(np.float64)
    b = np.arange(BEADS)[None, :].astype(np.float64)
    angle = 2.0 * math.pi * ((k * b) % BEADS) / BEADS
    scale = math.sqrt(2.0 / BEADS)
    basis = np.where(k < BEADS // 2, scale * np.cos(angle), scale * np.sin(angle))
    basis = np.where(k == 0, 1.0 / math.sqrt(BEADS), basis)
    basis = np.where(k == BEADS // 2, np.cos(math.pi * b) / math.sqrt(BEADS), basis)
    w = 2.0 * cycle_rate * np.sin(math.pi * np.arange(BEADS) / BEADS)
    ratio = np.where(w > 0, np.sin(w) / np.where(w > 0, w, 1.0), 1.0)
    columns = np.stack([np.cos(w), ratio, w * np.sin(w)], axis=1)

    def stacked(matrix):
        high = matrix.astype(jnp.bfloat16)
        low = (matrix - high.astype(np.float64)).astype(jnp.bfloat16)
        return np.concatenate([high, high, low], axis=1)

    matrices, tables = [], []
    for core in range(2):
        order = np.roll(np.arange(BEADS), -HALF * core)
        forward = basis[order][:, order]
        matrices.append(stacked(np.concatenate([forward, forward.T[:HALF]], axis=0)))
        tables.append(np.pad(columns[order], ((0, 0), (0, 5))))
    return np.stack(matrices), np.stack(tables).astype(np.float32)


MATRICES, TABLES = constants()


def call(body, outs, args, specs=None, out_specs=None, scratch=(), flops=0, nbytes=0, limit=24, alias=None):
    return pl.pallas_call(
        body,
        out_shape=outs,
        in_specs=specs or [VMEM] * len(args),
        out_specs=out_specs or [VMEM] * len(outs),
        scratch_shapes=scratch,
        input_output_aliases=alias or {},
        compiler_params=pltpu.CompilerParams(vmem_limit_bytes=limit << 20),
        cost_estimate=pl.CostEstimate(flops=flops, bytes_accessed=nbytes, transcendentals=0),
    )(*args)


def struct(*shape, dtype=F32):
    return jax.ShapeDtypeStruct(shape, dtype)


def shifted(array, axis, by):
    devices = lax.axis_size(axis)
    return lax.ppermute(array, axis, [(i, (i + by) % devices) for i in range(devices)])


def take(values, lanes):
    return lax.gather(
        values,
        lanes[..., None],
        lax.GatherDimensionNumbers(
            offset_dims=(),
            collapsed_slice_dims=(1,),
            start_index_map=(1,),
            operand_batching_dims=(0,),
            start_indices_batching_dims=(0,),
        ),
        slice_sizes=(1, 1),
        mode=lax.GatherScatterMode.PROMISE_IN_BOUNDS,
    )


def transform(matrix, values):
    high = values.astype(jnp.bfloat16)
    low = (values - high.astype(F32)).astype(jnp.bfloat16)
    return jnp.dot(matrix, jnp.concatenate([high, low, high], axis=0), preferred_element_type=F32)


def spread(row):
    return jnp.broadcast_to(row, (8, LANES))


def cols(tile):
    if isinstance(tile, int):
        return pl.ds(tile * LANES, LANES)
    return pl.ds(pl.multiple_of(tile * LANES, LANES), LANES)


def leavers(up_ref, down_ref):
    place = lax.broadcasted_iota(I32, (8, LANES), 1) & 15
    index = jnp.zeros((8, LANES), I32)
    for j in range(8):
        index = jnp.where(place == j, up_ref[j], index)
        index = jnp.where(place == 8 + j, down_ref[j], index)
    return index


def ahead():
    slab = lax.axis_index("space")
    way = 3 * (slab & 3) + 3 * (lax.shift_right_logical(slab, 2) & 3) + 5 * lax.shift_right_logical(slab, 4)
    return TILES - lax.shift_right_logical(way * TILES + HALF, 5)


def pick(load, high, low):
    found = take(load(0), low)
    for tile in range(1, TILES):
        found = jnp.where(high == tile, take(load(tile), low), found)
    return found


def make_lists(nbr_ref, rows_ref, words_ref):
    lane = lax.broadcasted_iota(I32, (SLOTS, LANES), 1)
    masks = []
    for tile in range(TILES):
        block = nbr_ref[:, cols(tile)]
        mine = lax.shift_left(jnp.ones_like(block), lax.shift_right_logical(block, 6))
        masks.append(jnp.where(block == lane + tile * LANES, 0, mine))
    for step, count in ((64, 4), (32, 2), (16, 1)):
        lower = (lane & step) == 0
        merged = []
        for at in range(count):
            first, second = masks[at], masks[at + count]
            other = jnp.where(lower, second, first)
            moved = jnp.where(lower, pltpu.roll(other, LANES - step, axis=1), pltpu.roll(other, step, axis=1))
            merged.append(jnp.where(lower, first, second) | moved)
        masks = merged
    bits = masks[0]
    for step in (8, 4, 2, 1):
        bits = bits | pltpu.roll(bits, LANES - step, axis=1)
    window = jnp.zeros_like(bits)
    wide = jnp.ones_like(bits)
    for at in range(WINDOWS):
        covered = sum(1 << ((at + i) % WINDOWS) for i in range(4))
        covered = covered - (1 << 32) if covered >= 1 << 31 else covered
        fits = (bits & ~covered) == 0
        window = jnp.where(fits, at, window)
        wide = jnp.where(fits, 0, wide)
    words_ref[...] = window | (wide << 8) | jnp.where(bits != 0, 1 << 9, 0)
    for tile in range(TILES):
        block = nbr_ref[:, cols(tile)]
        start = jnp.broadcast_to(window[:, 16 * tile:16 * tile + 1], (SLOTS, LANES)) << 6
        rows_ref[tile] = jnp.where(block == lane + tile * LANES, EMPTY, (block - start) & 2047)


def kick_body(therm_hbm, noise_hbm, drift_hbm, noisem_hbm, nbr_hbm, q_ref, therm_ref, noise_ref, coef_ref, rows_ref,
              words_ref, drift_ref, noisem_ref, nbr_ref, sems, small):
    def copies(pair):
        at = pl.ds(pl.multiple_of(pair * 2 * LANES, 2 * LANES), 2 * LANES)
        return (
            pltpu.make_async_copy(therm_hbm.at[:, :, at], therm_ref.at[:, :, at], sems.at[0, pair]),
            pltpu.make_async_copy(noise_hbm.at[:, :, at], noise_ref.at[:, :, at], sems.at[1, pair]),
        )

    matrices = (
        pltpu.make_async_copy(drift_hbm, drift_ref, small.at[0]),
        pltpu.make_async_copy(noisem_hbm, noisem_ref, small.at[1]),
        pltpu.make_async_copy(nbr_hbm, nbr_ref, small.at[2]),
    )
    for copy in matrices:
        copy.start()

    def begin(tile, carry):
        for copy in copies(tile):
            copy.start()
        return carry

    lax.fori_loop(0, TILES // 2, begin, 0)
    for copy in matrices:
        copy.wait()
    make_lists(nbr_ref, rows_ref, words_ref)
    for k in range(HALF):
        for at, ref in enumerate((drift_ref, noisem_ref)):
            block = ref[pl.ds(HALF + k, 8, stride=HALF), :]
            for j in range(9):
                coef_ref[k * 18 + at * 9 + j] = jnp.broadcast_to(block[:, j:j + 1], (8, LANES))
    d0, n0 = drift_ref[0:HALF, :], noisem_ref[0:HALF, :]
    q_ref[0:HALF, ATOMS:ATOMS + LANES] = jnp.broadcast_to(d0[:, 0:1], (HALF, LANES))
    q_ref[HALF:48, ATOMS:ATOMS + LANES] = jnp.zeros((48 - HALF, LANES), F32)
    ncol = [[jnp.broadcast_to(n0[g * 8:g * 8 + 8, j:j + 1], (8, LANES)) for j in range(9)] for g in range(2)]
    diagonal = lax.broadcasted_iota(I32, (8, 9), 1) == lax.broadcasted_iota(I32, (8, 9), 0) + 1
    dcol = []
    for k in range(HALF):
        row = jnp.where(diagonal, jnp.broadcast_to(d0[k:k + 1, :], (8, 9)), 0.0)
        dcol.append(jnp.broadcast_to(jnp.sum(row, axis=1, keepdims=True), (8, LANES)))
    sub = lax.broadcasted_iota(I32, (8, LANES), 0)
    m4, m2, m1 = sub < 4, (sub & 2) == 0, (sub & 1) == 0

    def tile_step(tile, carry):
        at = cols(tile)

        @pl.when((tile & 1) == 0)
        def _():
            for copy in copies(lax.shift_right_logical(tile, 1)):
                copy.wait()

        for c in range(3):
            for g in range(2):
                v = [therm_ref[(g * 8 + k) * 3 + c, :, at] * dcol[g * 8 + k] for k in range(8)]
                for mask, step, count in ((m4, 4, 4), (m2, 2, 2), (m1, 1, 1)):
                    merged = []
                    for k in range(count):
                        a, b = v[k], v[k + count]
                        z = jnp.where(mask, b, a)
                        if step == 4:
                            moved = pltpu.roll(z, 4, axis=0)
                        else:
                            moved = jnp.where(mask, pltpu.roll(z, 8 - step, axis=0), pltpu.roll(z, step, axis=0))
                        merged.append(jnp.where(mask, a, b) + moved)
                    v = merged
                total = v[0]
                for j in range(9):
                    total = total + ncol[g][j] * noise_ref[(j * 3 + c) * 2 + g, :, at]
                q_ref[pl.ds(c * HALF + g * 8, 8), at] = total
        return carry

    lax.fori_loop(0, TILES, tile_step, 0)


def modes_body(up_ref, down_ref, pos_ref, mom_ref, ppos_ref, pmom_ref, const_ref, therm_ref, noise_ref, coef_ref,
               modes_ref, part_ref, tcol, ncol):
    forward = const_ref[lax.axis_index("bead"), 0:BEADS, :]
    for c in range(3):
        r = slice(c * HALF, c * HALF + HALF)
        for at, (mine, other) in enumerate(((pos_ref, ppos_ref), (mom_ref, pmom_ref))):
            modes_ref[c, at] = transform(forward, jnp.concatenate([mine[r, :], other[r, :]], axis=0))
    leave = leavers(up_ref, down_ref)
    high, low = lax.shift_right_logical(leave, 7), leave & 127

    def therm_step(g, carry):
        tcol[g] = pick(lambda t: therm_ref[g, :, cols(t)], high, low)
        return carry

    def noise_step(g, carry):
        ncol[g] = pick(lambda t: noise_ref[g, :, cols(t)], high, low)
        return carry

    for g in range(48):
        therm_step(g, 0)
    for g in range(54):
        noise_step(g, 0)
    for k in range(HALF):
        for c in range(3):
            total = None
            for j in range(8):
                term = coef_ref[k * 18 + 1 + j] * spread(tcol[k * 3 + c, j:j + 1, :])
                total = term if total is None else total + term
            for j in range(9):
                row = spread(ncol[(j * 3 + c) * 2 + k // 8, k % 8:k % 8 + 1, :])
                total = total + coef_ref[k * 18 + 9 + j] * row
            part_ref[k * 3 + c] = total


def beads_body(up_ref, down_ref, modes_ref, q_ref, pq_ref, const_ref, table_ref, part_ref, coef_ref, gup_ref, gdown_ref,
               pos_ref, mom_ref, mm_ref, ubuf_ref, dbuf_ref, upack_ref, dpack_ref, codes_ref, packs):
    core = lax.axis_index("bead")
    table = table_ref[core]
    d00 = jnp.concatenate([q_ref[0:HALF, ATOMS:ATOMS + 1], pq_ref[0:HALF, ATOMS:ATOMS + 1]], axis=0)
    cosine, ratio, stiff = table[:, 0:1], table[:, 1:2], table[:, 2:3]
    backward = const_ref[core, 32:48, :]
    for c in range(3):
        r = slice(c * HALF, c * HALF + HALF)
        mode_pos, mode_mom = modes_ref[c, 0], modes_ref[c, 1]
        kicked = d00 * mode_mom + jnp.concatenate([q_ref[r, 0:ATOMS], pq_ref[r, 0:ATOMS]], axis=0)
        free_pos = cosine * mode_pos + ratio * kicked
        free_mom = cosine * kicked - stiff * mode_pos
        pos_ref[r, :] = transform(backward, free_pos)
        mom_ref[r, :] = transform(backward, free_mom)
        mm_ref[r, :] = mode_mom[0:HALF]

    for buf, ghost_ref in ((ubuf_ref, gup_ref), (dbuf_ref, gdown_ref)):
        for tile in range(GHOST_TILES):
            index = jnp.broadcast_to(ghost_ref[tile * LANES:tile * LANES + LANES].reshape(1, LANES), (8, LANES))
            high, low = lax.shift_right_logical(index, 7), index & 127
            for g in range(6):
                at = tile * 48 + g * 8
                buf[at:at + 8, :] = pick(lambda t: pos_ref[g * 8:g * 8 + 8, cols(t)], high, low)
            code = jnp.full((8, LANES), -1.0, F32)
            for j in range(8):
                code = jnp.where(index == up_ref[j], 8.0 + j, code)
                code = jnp.where(index == down_ref[j], 0.0 + j, code)
            buf[256 + tile:257 + tile, :] = code[0:1, :]
        buf[260:264, :] = jnp.zeros((4, LANES), F32)

    leave = leavers(up_ref, down_ref)
    high, low = lax.shift_right_logical(leave, 7), leave & 127
    group = lax.shift_right_logical(lax.broadcasted_iota(I32, (8, LANES), 1), 4)
    packed = [jnp.zeros((8, LANES), F32) for _ in range(8)]

    def put(at, value):
        packed[at // 8] = jnp.where(group == at % 8, value, packed[at // 8])

    for g in range(6):
        put(g, pick(lambda t: pos_ref[g * 8:g * 8 + 8, cols(t)], high, low))
        put(6 + g, pick(lambda t: mom_ref[g * 8:g * 8 + 8, cols(t)], high, low))
        packs[g] = pick(lambda t: mm_ref[g * 8:g * 8 + 8, cols(t)], high, low)
    for k in range(HALF):
        column = coef_ref[k * 18]
        for c in range(3):
            row = spread(packs[c * 2 + k // 8, k % 8:k % 8 + 1, :])
            put(12 + k * 3 + c, part_ref[k * 3 + c] + column * row)
    for buf in (ubuf_ref, dbuf_ref):
        for at in range(8):
            buf[192 + at * 8:200 + at * 8, :] = packed[at]
    upack_ref[...] = packed[0]
    dpack_ref[...] = packed[0]
    at = lax.broadcasted_iota(I32, (8, LANES), 0) * LANES + lax.broadcasted_iota(I32, (8, LANES), 1)
    code = jnp.full((8, LANES), -1, I32)
    for j in range(8):
        code = jnp.where(at == up_ref[j], 8 + j, code)
        code = jnp.where(at == down_ref[j], j, code)
    codes_ref[...] = code


def aux_work(first, last, therm_ref, noise_ref, mm_ref, coef_ref, aux_ref):
    def tile_step(tile, carry):
        at = cols(tile)
        for k in range(HALF):
            column = [coef_ref[k * 18 + j] for j in range(18)]
            for c in range(3):
                row = c * HALF + k
                total = column[0] * spread(mm_ref[row:row + 1, at])
                for j in range(8):
                    total = total + column[1 + j] * spread(therm_ref[k * 3 + c, j:j + 1, at])
                for j in range(9):
                    total = total + column[9 + j] * spread(noise_ref[(j * 3 + c) * 2 + k // 8, k % 8:k % 8 + 1, at])
                aux_ref[k * 3 + c, :, at] = total
        return carry

    lax.fori_loop(first, last, tile_step, 0)


def aux_first(therm_ref, noise_ref, mm_ref, coef_ref, buf_in, pack_in, aux_ref, buf_out, pack_out):
    aux_work(0, ahead(), therm_ref, noise_ref, mm_ref, coef_ref, aux_ref)


def aux_second(done_ref, therm_ref, noise_ref, mm_ref, coef_ref, aux_ref):
    aux_work(ahead(), TILES, therm_ref, noise_ref, mm_ref, coef_ref, aux_ref)


def force_body(words_vmem, codes, nbr_ref, pos_ref, mom_ref, aux_ref, pack_ref, low_ref, high_ref,
               low2_ref, high2_ref, moved_hbm, momout_hbm, auxout_hbm, table, aux, moved_ref, momout_ref, came_ref, words_ref,
               sems, tile_sems):
    fetch = pltpu.make_async_copy(words_vmem, words_ref, sems.at[0])
    fetch.start()
    lane = lax.broadcasted_iota(I32, (8, LANES), 1)
    from_low = (lane & 15) < 8

    def turned(value, place):
        return pltpu.roll(value, LANES - 16 * place, axis=1) if place else value

    for at in range(8):
        r = slice(192 + at * 8, 200 + at * 8)
        packed = jnp.where(from_low, low_ref[r, :], high_ref[r, :])
        for place in range(8 if at < 7 else 4):
            came_ref[at * 8 + place] = turned(packed, place)

    def own_tile(tile, carry):
        at = cols(tile)
        mine = spread(codes[pl.ds(tile, 1), :])
        comes, base = mine >= 0, jnp.maximum(mine, 0)
        for g in range(6):
            r = slice(g * 8, g * 8 + 8)
            new = jnp.where(comes, take(came_ref[g], base), pos_ref[r, at])
            table[2 * tile, r, :] = new
            moved_ref[r, at] = new
            momout_ref[r, at] = jnp.where(comes, take(came_ref[6 + g], base), mom_ref[r, at])
        for g in range(48):
            aux[g, :, at] = jnp.where(comes, take(came_ref[12 + g], base), aux_ref[g, :, at])
        return carry

    lax.fori_loop(0, TILES, own_tile, 0, unroll=2)
    outs = (
        pltpu.make_async_copy(moved_ref, moved_hbm, sems.at[1]),
        pltpu.make_async_copy(aux, auxout_hbm, sems.at[2]),
    )
    for out in outs:
        out.start()

    for side, (buf, source) in enumerate((
        (low_ref, jnp.where(from_low, low2_ref[...], pack_ref[...])),
        (high_ref, jnp.where(from_low, pack_ref[...], high2_ref[...])),
    )):
        sources = [turned(source, g) for g in range(6)]
        for tile in range(GHOST_TILES):
            row = 256 + tile
            mine = spread(buf[row:row + 1, :]).astype(I32)
            comes, base = mine >= 0, jnp.maximum(mine, 0)
            for g in range(6):
                r = slice(g * 8, g * 8 + 8)
                old = buf[tile * 48 + g * 8:tile * 48 + g * 8 + 8, :]
                table[2 * (TILES + side * GHOST_TILES + tile), r, :] = jnp.where(comes, take(sources[g], base), old)

    for g in range(6):
        r = slice(g * 8, g * 8 + 8)
        rolled = [pltpu.roll(table[2 * tile, r, :], 64, axis=1) for tile in range(2 * TILES)]
        for tile in range(2 * TILES):
            table[2 * tile + 1, r, :] = jnp.where(lane < 64, rolled[tile], rolled[(tile + 1) % (2 * TILES)])
    fetch.wait()

    def leave(tile):
        at = cols(tile)
        return pltpu.make_async_copy(momout_ref.at[:, at], momout_hbm.at[:, at], tile_sems.at[tile])

    def atom_tile(tile, carry):
        at = cols(tile)
        own = [table[2 * tile, g * 8:g * 8 + 8, :] for g in range(6)]

        def pull(found, hit, low, place):
            return [jnp.where(hit, take(table[place, g * 8:g * 8 + 8, :], low), found[g]) for g in range(6)]

        def push(total, found):
            done = list(total)
            for half in range(2):
                d = [own[2 * c + half] - found[2 * c + half] for c in range(3)]
                weight = jnp.exp((d[0] * d[0] + d[1] * d[1] + d[2] * d[2]) * (-0.5 / core_width))
                for c in range(3):
                    done[2 * c + half] = done[2 * c + half] + d[c] * weight
            return tuple(done)

        def chunk(number, total):
            first = number * CHUNK
            words = [words_ref[first + u, 16 * tile] for u in range(CHUNK)]
            seen = words[0]
            for word in words[1:]:
                seen = seen | word

            def fast(total):
                for u in range(CHUNK):
                    index = spread(nbr_ref[tile, pl.ds(first + u, 1), :])
                    high, low = lax.shift_right_logical(index, 7), index & 127
                    place = words[u] & 31
                    found = pull(own, high == 0, low, place)
                    total = push(total, pull(found, high == 1, low, (place + 2) & 31))
                return total

            def slow(total):
                def one(u, total):
                    index = spread(nbr_ref[tile, pl.ds(first + u, 1), :])
                    index = jnp.where(index == EMPTY, EMPTY, (index + (words_ref[first + u, 16 * tile] & 31) * 64) & 2047)
                    high, low = lax.shift_right_logical(index, 7), index & 127
                    found = lax.fori_loop(
                        0, 16, lambda place, found: tuple(pull(found, high == place, low, 2 * place)), tuple(own)
                    )
                    return push(total, found)

                return lax.fori_loop(0, CHUNK, one, total)

            def some(total):
                return lax.cond((seen & (1 << 8)) != 0, slow, fast, total)

            return lax.cond((seen & (1 << 9)) != 0, some, lambda total: total, total)

        zero = jnp.zeros((8, LANES), F32)
        total = lax.fori_loop(0, SLOTS // CHUNK, chunk, (zero,) * 6)
        for g in range(6):
            r = slice(g * 8, g * 8 + 8)
            momout_ref[r, at] = momout_ref[r, at] + kick_scale * total[g]
        leave(tile).start()
        return carry

    lax.fori_loop(0, TILES, atom_tile, 0)
    for out in outs:
        out.wait()
    for tile in range(TILES):
        leave(tile).wait()


def per_device(positions, momenta, thermostat, white_noise, drift_matrix, noise_matrix, leave_up, leave_down,
               ghost_up, ghost_down, neighbours):
    pos = positions.transpose(1, 0, 2).reshape(48, ATOMS)
    mom = momenta.transpose(1, 0, 2).reshape(48, ATOMS)
    therm = thermostat.transpose(0, 2, 1, 3).reshape(48, 8, ATOMS)
    noise = white_noise.transpose(1, 2, 0, 3).reshape(54, 8, ATOMS)
    drift = drift_matrix.transpose(1, 0, 2).reshape(144, 9)
    noisem = noise_matrix.transpose(1, 0, 2).reshape(144, 9)
    matrices, tables = jnp.asarray(MATRICES), jnp.asarray(TABLES)

    other_pos = shifted(pos, "bead", 1)
    other_mom = shifted(mom, "bead", 1)
    held = [pltpu.with_memory_space_constraint(x, pltpu.HBM) for x in (therm, noise, drift, noisem, neighbours)]
    q, therm, noise, coef, rows, words = call(
        kick_body,
        [
            struct(48, ATOMS + LANES), struct(48, 8, ATOMS), struct(54, 8, ATOMS), struct(288, 8, LANES),
            struct(TILES, SLOTS, LANES, dtype=I32), struct(SLOTS, LANES, dtype=I32),
        ],
        held, specs=[HBM] * 5,
        scratch=[
            pltpu.VMEM((144, 9), F32), pltpu.VMEM((144, 9), F32), pltpu.VMEM((SLOTS, ATOMS), I32),
            pltpu.SemaphoreType.DMA((2, TILES)), pltpu.SemaphoreType.DMA((3,)),
        ],
        flops=4000000, nbytes=3600000,
    )
    other_q = shifted(q, "bead", 1)
    modes, part = call(
        modes_body,
        [struct(3, 2, BEADS, ATOMS), struct(48, 8, LANES)],
        [leave_up, leave_down, pos, mom, other_pos, other_mom, matrices, therm, noise, coef],
        specs=[SMEM] * 2 + [VMEM] * 8,
        scratch=[pltpu.VMEM((48, 8, LANES), F32), pltpu.VMEM((54, 8, LANES), F32)],
        flops=8000000, nbytes=4000000,
    )
    bead_pos, bead_mom, mode_mom, up_buf, down_buf, up_pack, down_pack, codes = call(
        beads_body,
        [struct(48, ATOMS)] * 3 + [struct(264, LANES)] * 2 + [struct(8, LANES)] * 2 + [struct(8, LANES, dtype=I32)],
        [leave_up, leave_down, modes, q, other_q, matrices, tables, part, coef, ghost_up, ghost_down],
        specs=[SMEM] * 2 + [VMEM] * 9,
        scratch=[pltpu.VMEM((6, 8, LANES), F32)],
        flops=8000000, nbytes=2000000,
    )
    low = shifted(up_buf, "space", 1)
    low2 = shifted(up_pack, "space", 2)
    work = [therm, noise, mode_mom, coef]
    aux, down_buf, down_pack = call(
        aux_first, [struct(48, 8, ATOMS), struct(264, LANES), struct(8, LANES)], work + [down_buf, down_pack],
        specs=[VMEM] * 4 + [ANY] * 2, out_specs=[VMEM, ANY, ANY], alias={4: 1, 5: 2}, flops=1000, nbytes=1000,
    )
    high = shifted(down_buf, "space", -1)
    high2 = shifted(down_pack, "space", -2)
    (aux,) = call(aux_second, [struct(48, 8, ATOMS)], [aux] + work, alias={0: 0}, flops=16000000, nbytes=5000000)
    moved, slab, out_aux = call(
        force_body,
        [struct(48, ATOMS), struct(48, ATOMS), struct(48, 8, ATOMS)],
        [words, codes, rows, bead_pos, bead_mom, aux, up_pack, low, high, low2, high2],
        out_specs=[HBM] * 3,
        scratch=[
            pltpu.VMEM((WINDOWS, 48, LANES), F32),
            pltpu.VMEM((48, 8, ATOMS), F32),
            pltpu.VMEM((48, ATOMS), F32),
            pltpu.VMEM((48, ATOMS), F32),
            pltpu.VMEM((60, 8, LANES), F32),
            pltpu.SMEM((SLOTS, LANES), I32),
            pltpu.SemaphoreType.DMA((3,)),
            pltpu.SemaphoreType.DMA((TILES,)),
        ],
        flops=30000000, nbytes=4000000,
    )
    moved = moved.reshape(3, HALF, ATOMS).transpose(1, 0, 2)
    slab = slab.reshape(3, HALF, ATOMS).transpose(1, 0, 2)
    out_aux = out_aux.reshape(HALF, 3, 8, ATOMS).transpose(0, 2, 1, 3)
    return (moved, slab, out_aux)


def solution(mesh):
    in_specs = (
        P("bead", None, "space"),
        P("bead", None, "space"),
        P("bead", None, None, "space"),
        P("bead", None, None, "space"),
        P("bead", None, None),
        P("bead", None, None),
        P("space"),
        P("space"),
        P("space"),
        P("space"),
        P(None, "space"),
    )
    out_specs = (P("bead", None, "space"), P("bead", None, "space"), P("bead", None, None, "space"))

    return jax.shard_map(per_device, mesh=mesh, in_specs=in_specs, out_specs=out_specs, check_vma=False)
```

```python
import math

import jax
import jax.numpy as jnp
import numpy as np
from jax import lax
from jax.experimental import pallas as pl
from jax.experimental.pallas import tpu as pltpu
from jax.sharding import PartitionSpec as P


BEADS = 32
HALF = 16
ATOMS = 1024
TILES = 8
SLOTS = 32
GHOST_TILES = 4
LANES = 128
WINDOWS = 32
EMPTY = 4095
CHUNK = 32

cycle_rate = 0.8
kick_scale = 0.2
core_width = 4.0

F32 = jnp.float32
I32 = jnp.int32
VMEM = pl.BlockSpec(memory_space=pltpu.VMEM)
SMEM = pl.BlockSpec(memory_space=pltpu.SMEM)
ANY = pl.BlockSpec(memory_space=pl.ANY)
HBM = pl.BlockSpec(memory_space=pltpu.HBM)


def constants():
    k = np.arange(BEADS)[:, None].astype(np.float64)
    b = np.arange(BEADS)[None, :].astype(np.float64)
    angle = 2.0 * math.pi * ((k * b) % BEADS) / BEADS
    scale = math.sqrt(2.0 / BEADS)
    basis = np.where(k < BEADS // 2, scale * np.cos(angle), scale * np.sin(angle))
    basis = np.where(k == 0, 1.0 / math.sqrt(BEADS), basis)
    basis = np.where(k == BEADS // 2, np.cos(math.pi * b) / math.sqrt(BEADS), basis)
    w = 2.0 * cycle_rate * np.sin(math.pi * np.arange(BEADS) / BEADS)
    ratio = np.where(w > 0, np.sin(w) / np.where(w > 0, w, 1.0), 1.0)
    columns = np.stack([np.cos(w), ratio, w * np.sin(w)], axis=1)

    def stacked(matrix):
        high = matrix.astype(jnp.bfloat16)
        low = (matrix - high.astype(np.float64)).astype(jnp.bfloat16)
        return np.concatenate([high, high, low], axis=1)

    matrices, tables = [], []
    for core in range(2):
        order = np.roll(np.arange(BEADS), -HALF * core)
        forward = basis[order][:, order]
        matrices.append(stacked(np.concatenate([forward, forward.T[:HALF]], axis=0)))
        tables.append(np.pad(columns[order], ((0, 0), (0, 5))))
    return np.stack(matrices), np.stack(tables).astype(np.float32)


MATRICES, TABLES = constants()


def call(body, outs, args, specs=None, out_specs=None, scratch=(), flops=0, nbytes=0, limit=24, alias=None):
    return pl.pallas_call(
        body,
        out_shape=outs,
        in_specs=specs or [VMEM] * len(args),
        out_specs=out_specs or [VMEM] * len(outs),
        scratch_shapes=scratch,
        input_output_aliases=alias or {},
        compiler_params=pltpu.CompilerParams(vmem_limit_bytes=limit << 20),
        cost_estimate=pl.CostEstimate(flops=flops, bytes_accessed=nbytes, transcendentals=0),
    )(*args)


def struct(*shape, dtype=F32):
    return jax.ShapeDtypeStruct(shape, dtype)


def shifted(array, axis, by):
    devices = lax.axis_size(axis)
    return lax.ppermute(array, axis, [(i, (i + by) % devices) for i in range(devices)])


def take(values, lanes):
    return lax.gather(
        values,
        lanes[..., None],
        lax.GatherDimensionNumbers(
            offset_dims=(),
            collapsed_slice_dims=(1,),
            start_index_map=(1,),
            operand_batching_dims=(0,),
            start_indices_batching_dims=(0,),
        ),
        slice_sizes=(1, 1),
        mode=lax.GatherScatterMode.PROMISE_IN_BOUNDS,
    )


def transform(matrix, values):
    high = values.astype(jnp.bfloat16)
    low = (values - high.astype(F32)).astype(jnp.bfloat16)
    return jnp.dot(matrix, jnp.concatenate([high, low, high], axis=0), preferred_element_type=F32)


def spread(row):
    return jnp.broadcast_to(row, (8, LANES))


def cols(tile):
    if isinstance(tile, int):
        return pl.ds(tile * LANES, LANES)
    return pl.ds(pl.multiple_of(tile * LANES, LANES), LANES)


def leavers(up_ref, down_ref):
    place = lax.broadcasted_iota(I32, (8, LANES), 1) & 15
    index = jnp.zeros((8, LANES), I32)
    for j in range(8):
        index = jnp.where(place == j, up_ref[j], index)
        index = jnp.where(place == 8 + j, down_ref[j], index)
    return index


def ahead():
    slab = lax.axis_index("space")
    way = 3 * (slab & 3) + 3 * (lax.shift_right_logical(slab, 2) & 3) + 5 * lax.shift_right_logical(slab, 4)
    return TILES - lax.shift_right_logical(way * TILES + HALF, 5)


def pick(load, high, low):
    found = take(load(0), low)
    for tile in range(1, TILES):
        found = jnp.where(high == tile, take(load(tile), low), found)
    return found


def make_lists(nbr_ref, rows_ref, words_ref):
    lane = lax.broadcasted_iota(I32, (SLOTS, LANES), 1)
    masks = []
    for tile in range(TILES):
        block = nbr_ref[:, cols(tile)]
        mine = lax.shift_left(jnp.ones_like(block), lax.shift_right_logical(block, 6))
        masks.append(jnp.where(block == lane + tile * LANES, 0, mine))
    for step, count in ((64, 4), (32, 2), (16, 1)):
        lower = (lane & step) == 0
        merged = []
        for at in range(count):
            first, second = masks[at], masks[at + count]
            other = jnp.where(lower, second, first)
            moved = jnp.where(lower, pltpu.roll(other, LANES - step, axis=1), pltpu.roll(other, step, axis=1))
            merged.append(jnp.where(lower, first, second) | moved)
        masks = merged
    bits = masks[0]
    for step in (8, 4, 2, 1):
        bits = bits | pltpu.roll(bits, LANES - step, axis=1)
    window = jnp.zeros_like(bits)
    wide = jnp.ones_like(bits)
    for at in range(WINDOWS):
        covered = sum(1 << ((at + i) % WINDOWS) for i in range(4))
        covered = covered - (1 << 32) if covered >= 1 << 31 else covered
        fits = (bits & ~covered) == 0
        window = jnp.where(fits, at, window)
        wide = jnp.where(fits, 0, wide)
    words_ref[...] = window | (wide << 8) | jnp.where(bits != 0, 1 << 9, 0)
    for tile in range(TILES):
        block = nbr_ref[:, cols(tile)]
        start = jnp.broadcast_to(window[:, 16 * tile:16 * tile + 1], (SLOTS, LANES)) << 6
        rows_ref[tile] = jnp.where(block == lane + tile * LANES, EMPTY, (block - start) & 2047)


def kick_body(therm_hbm, noise_hbm, drift_hbm, noisem_hbm, nbr_hbm, q_ref, therm_ref, noise_ref, coef_ref, rows_ref,
              words_ref, drift_ref, noisem_ref, nbr_ref, sems, small):
    def copies(pair):
        at = pl.ds(pl.multiple_of(pair * 2 * LANES, 2 * LANES), 2 * LANES)
        return (
            pltpu.make_async_copy(therm_hbm.at[:, :, at], therm_ref.at[:, :, at], sems.at[0, pair]),
            pltpu.make_async_copy(noise_hbm.at[:, :, at], noise_ref.at[:, :, at], sems.at[1, pair]),
        )

    matrices = (
        pltpu.make_async_copy(drift_hbm, drift_ref, small.at[0]),
        pltpu.make_async_copy(noisem_hbm, noisem_ref, small.at[1]),
        pltpu.make_async_copy(nbr_hbm, nbr_ref, small.at[2]),
    )
    for copy in matrices:
        copy.start()

    def begin(tile, carry):
        for copy in copies(tile):
            copy.start()
        return carry

    lax.fori_loop(0, TILES // 2, begin, 0)
    for copy in matrices:
        copy.wait()
    make_lists(nbr_ref, rows_ref, words_ref)
    for k in range(HALF):
        for at, ref in enumerate((drift_ref, noisem_ref)):
            block = ref[pl.ds(HALF + k, 8, stride=HALF), :]
            for j in range(9):
                coef_ref[k * 18 + at * 9 + j] = jnp.broadcast_to(block[:, j:j + 1], (8, LANES))
    d0, n0 = drift_ref[0:HALF, :], noisem_ref[0:HALF, :]
    q_ref[0:HALF, ATOMS:ATOMS + LANES] = jnp.broadcast_to(d0[:, 0:1], (HALF, LANES))
    q_ref[HALF:48, ATOMS:ATOMS + LANES] = jnp.zeros((48 - HALF, LANES), F32)
    ncol = [[jnp.broadcast_to(n0[g * 8:g * 8 + 8, j:j + 1], (8, LANES)) for j in range(9)] for g in range(2)]
    diagonal = lax.broadcasted_iota(I32, (8, 9), 1) == lax.broadcasted_iota(I32, (8, 9), 0) + 1
    dcol = []
    for k in range(HALF):
        row = jnp.where(diagonal, jnp.broadcast_to(d0[k:k + 1, :], (8, 9)), 0.0)
        dcol.append(jnp.broadcast_to(jnp.sum(row, axis=1, keepdims=True), (8, LANES)))
    sub = lax.broadcasted_iota(I32, (8, LANES), 0)
    m4, m2, m1 = sub < 4, (sub & 2) == 0, (sub & 1) == 0

    def tile_step(tile, carry):
        at = cols(tile)

        @pl.when((tile & 1) == 0)
        def _():
            for copy in copies(lax.shift_right_logical(tile, 1)):
                copy.wait()

        for c in range(3):
            for g in range(2):
                v = [therm_ref[(g * 8 + k) * 3 + c, :, at] * dcol[g * 8 + k] for k in range(8)]
                for mask, step, count in ((m4, 4, 4), (m2, 2, 2), (m1, 1, 1)):
                    merged = []
                    for k in range(count):
                        a, b = v[k], v[k + count]
                        z = jnp.where(mask, b, a)
                        if step == 4:
                            moved = pltpu.roll(z, 4, axis=0)
                        else:
                            moved = jnp.where(mask, pltpu.roll(z, 8 - step, axis=0), pltpu.roll(z, step, axis=0))
                        merged.append(jnp.where(mask, a, b) + moved)
                    v = merged
                total = v[0]
                for j in range(9):
                    total = total + ncol[g][j] * noise_ref[(j * 3 + c) * 2 + g, :, at]
                q_ref[pl.ds(c * HALF + g * 8, 8), at] = total
        return carry

    lax.fori_loop(0, TILES, tile_step, 0)


def modes_body(up_ref, down_ref, pos_ref, mom_ref, ppos_ref, pmom_ref, const_ref, therm_ref, noise_ref, coef_ref,
               modes_ref, part_ref, tcol, ncol):
    forward = const_ref[lax.axis_index("bead"), 0:BEADS, :]
    for c in range(3):
        r = slice(c * HALF, c * HALF + HALF)
        for at, (mine, other) in enumerate(((pos_ref, ppos_ref), (mom_ref, pmom_ref))):
            modes_ref[c, at] = transform(forward, jnp.concatenate([mine[r, :], other[r, :]], axis=0))
    leave = leavers(up_ref, down_ref)
    high, low = lax.shift_right_logical(leave, 7), leave & 127

    def therm_step(g, carry):
        tcol[g] = pick(lambda t: therm_ref[g, :, cols(t)], high, low)
        return carry

    def noise_step(g, carry):
        ncol[g] = pick(lambda t: noise_ref[g, :, cols(t)], high, low)
        return carry

    for g in range(48):
        therm_step(g, 0)
    for g in range(54):
        noise_step(g, 0)
    for k in range(HALF):
        for c in range(3):
            total = None
            for j in range(8):
                term = coef_ref[k * 18 + 1 + j] * spread(tcol[k * 3 + c, j:j + 1, :])
                total = term if total is None else total + term
            for j in range(9):
                row = spread(ncol[(j * 3 + c) * 2 + k // 8, k % 8:k % 8 + 1, :])
                total = total + coef_ref[k * 18 + 9 + j] * row
            part_ref[k * 3 + c] = total


def beads_body(up_ref, down_ref, modes_ref, q_ref, pq_ref, const_ref, table_ref, part_ref, coef_ref, gup_ref, gdown_ref,
               pos_ref, mom_ref, mm_ref, ubuf_ref, dbuf_ref, upack_ref, dpack_ref, codes_ref, packs):
    core = lax.axis_index("bead")
    table = table_ref[core]
    d00 = jnp.concatenate([q_ref[0:HALF, ATOMS:ATOMS + 1], pq_ref[0:HALF, ATOMS:ATOMS + 1]], axis=0)
    cosine, ratio, stiff = table[:, 0:1], table[:, 1:2], table[:, 2:3]
    backward = const_ref[core, 32:48, :]
    for c in range(3):
        r = slice(c * HALF, c * HALF + HALF)
        mode_pos, mode_mom = modes_ref[c, 0], modes_ref[c, 1]
        kicked = d00 * mode_mom + jnp.concatenate([q_ref[r, 0:ATOMS], pq_ref[r, 0:ATOMS]], axis=0)
        free_pos = cosine * mode_pos + ratio * kicked
        free_mom = cosine * kicked - stiff * mode_pos
        pos_ref[r, :] = transform(backward, free_pos)
        mom_ref[r, :] = transform(backward, free_mom)
        mm_ref[r, :] = mode_mom[0:HALF]

    for buf, ghost_ref in ((ubuf_ref, gup_ref), (dbuf_ref, gdown_ref)):
        for tile in range(GHOST_TILES):
            index = jnp.broadcast_to(ghost_ref[tile * LANES:tile * LANES + LANES].reshape(1, LANES), (8, LANES))
            high, low = lax.shift_right_logical(index, 7), index & 127
            for g in range(6):
                at = tile * 48 + g * 8
                buf[at:at + 8, :] = pick(lambda t: pos_ref[g * 8:g * 8 + 8, cols(t)], high, low)
            code = jnp.full((8, LANES), -1.0, F32)
            for j in range(8):
                code = jnp.where(index == up_ref[j], 8.0 + j, code)
                code = jnp.where(index == down_ref[j], 0.0 + j, code)
            buf[256 + tile:257 + tile, :] = code[0:1, :]
        buf[260:264, :] = jnp.zeros((4, LANES), F32)

    leave = leavers(up_ref, down_ref)
    high, low = lax.shift_right_logical(leave, 7), leave & 127
    group = lax.shift_right_logical(lax.broadcasted_iota(I32, (8, LANES), 1), 4)
    packed = [jnp.zeros((8, LANES), F32) for _ in range(8)]

    def put(at, value):
        packed[at // 8] = jnp.where(group == at % 8, value, packed[at // 8])

    for g in range(6):
        put(g, pick(lambda t: pos_ref[g * 8:g * 8 + 8, cols(t)], high, low))
        put(6 + g, pick(lambda t: mom_ref[g * 8:g * 8 + 8, cols(t)], high, low))
        packs[g] = pick(lambda t: mm_ref[g * 8:g * 8 + 8, cols(t)], high, low)
    for k in range(HALF):
        column = coef_ref[k * 18]
        for c in range(3):
            row = spread(packs[c * 2 + k // 8, k % 8:k % 8 + 1, :])
            put(12 + k * 3 + c, part_ref[k * 3 + c] + column * row)
    for buf in (ubuf_ref, dbuf_ref):
        for at in range(8):
            buf[192 + at * 8:200 + at * 8, :] = packed[at]
    upack_ref[...] = packed[0]
    dpack_ref[...] = packed[0]
    at = lax.broadcasted_iota(I32, (8, LANES), 0) * LANES + lax.broadcasted_iota(I32, (8, LANES), 1)
    code = jnp.full((8, LANES), -1, I32)
    for j in range(8):
        code = jnp.where(at == up_ref[j], 8 + j, code)
        code = jnp.where(at == down_ref[j], j, code)
    codes_ref[...] = code


def aux_work(first, last, therm_ref, noise_ref, mm_ref, coef_ref, aux_ref):
    def tile_step(tile, carry):
        at = cols(tile)
        for k in range(HALF):
            column = [coef_ref[k * 18 + j] for j in range(18)]
            for c in range(3):
                row = c * HALF + k
                total = column[0] * spread(mm_ref[row:row + 1, at])
                for j in range(8):
                    total = total + column[1 + j] * spread(therm_ref[k * 3 + c, j:j + 1, at])
                for j in range(9):
                    total = total + column[9 + j] * spread(noise_ref[(j * 3 + c) * 2 + k // 8, k % 8:k % 8 + 1, at])
                aux_ref[k * 3 + c, :, at] = total
        return carry

    lax.fori_loop(first, last, tile_step, 0)


def aux_first(therm_ref, noise_ref, mm_ref, coef_ref, buf_in, pack_in, aux_ref, buf_out, pack_out):
    aux_work(0, ahead(), therm_ref, noise_ref, mm_ref, coef_ref, aux_ref)


def aux_second(done_ref, therm_ref, noise_ref, mm_ref, coef_ref, aux_ref):
    aux_work(ahead(), TILES, therm_ref, noise_ref, mm_ref, coef_ref, aux_ref)


def force_body(words_vmem, codes, nbr_ref, pos_ref, mom_ref, aux_ref, pack_ref, low_ref, high_ref,
               low2_ref, high2_ref, moved_hbm, momout_hbm, auxout_hbm, table, aux, moved_ref, momout_ref, came_ref, words_ref,
               sems, tile_sems):
    fetch = pltpu.make_async_copy(words_vmem, words_ref, sems.at[0])
    fetch.start()
    lane = lax.broadcasted_iota(I32, (8, LANES), 1)
    from_low = (lane & 15) < 8

    def turned(value, place):
        return pltpu.roll(value, LANES - 16 * place, axis=1) if place else value

    for at in range(8):
        r = slice(192 + at * 8, 200 + at * 8)
        packed = jnp.where(from_low, low_ref[r, :], high_ref[r, :])
        for place in range(8 if at < 7 else 4):
            came_ref[at * 8 + place] = turned(packed, place)

    def own_tile(tile, carry):
        at = cols(tile)
        mine = spread(codes[pl.ds(tile, 1), :])
        comes, base = mine >= 0, jnp.maximum(mine, 0)
        for g in range(6):
            r = slice(g * 8, g * 8 + 8)
            new = jnp.where(comes, take(came_ref[g], base), pos_ref[r, at])
            table[2 * tile, r, :] = new
            moved_ref[r, at] = new
            momout_ref[r, at] = jnp.where(comes, take(came_ref[6 + g], base), mom_ref[r, at])
        for g in range(48):
            aux[g, :, at] = jnp.where(comes, take(came_ref[12 + g], base), aux_ref[g, :, at])
        return carry

    lax.fori_loop(0, TILES, own_tile, 0, unroll=2)
    outs = (
        pltpu.make_async_copy(moved_ref, moved_hbm, sems.at[1]),
        pltpu.make_async_copy(aux, auxout_hbm, sems.at[2]),
    )
    for out in outs:
        out.start()

    for side, (buf, source) in enumerate((
        (low_ref, jnp.where(from_low, low2_ref[...], pack_ref[...])),
        (high_ref, jnp.where(from_low, pack_ref[...], high2_ref[...])),
    )):
        sources = [turned(source, g) for g in range(6)]
        for tile in range(GHOST_TILES):
            row = 256 + tile
            mine = spread(buf[row:row + 1, :]).astype(I32)
            comes, base = mine >= 0, jnp.maximum(mine, 0)
            for g in range(6):
                r = slice(g * 8, g * 8 + 8)
                old = buf[tile * 48 + g * 8:tile * 48 + g * 8 + 8, :]
                table[2 * (TILES + side * GHOST_TILES + tile), r, :] = jnp.where(comes, take(sources[g], base), old)

    for g in range(6):
        r = slice(g * 8, g * 8 + 8)
        rolled = [pltpu.roll(table[2 * tile, r, :], 64, axis=1) for tile in range(2 * TILES)]
        for tile in range(2 * TILES):
            table[2 * tile + 1, r, :] = jnp.where(lane < 64, rolled[tile], rolled[(tile + 1) % (2 * TILES)])
    fetch.wait()

    def leave(tile):
        at = cols(tile)
        return pltpu.make_async_copy(momout_ref.at[:, at], momout_hbm.at[:, at], tile_sems.at[tile])

    def atom_tile(tile, carry):
        at = cols(tile)
        own = [table[2 * tile, g * 8:g * 8 + 8, :] for g in range(6)]

        def pull(found, hit, low, place):
            return [jnp.where(hit, take(table[place, g * 8:g * 8 + 8, :], low), found[g]) for g in range(6)]

        def push(total, found, valid=None):
            done = list(total)
            for half in range(2):
                d = [own[2 * c + half] - found[2 * c + half] for c in range(3)]
                weight = jnp.exp2((d[0] * d[0] + d[1] * d[1] + d[2] * d[2]) * (-0.5 / core_width / math.log(2.0)))
                if valid is not None:
                    weight = jnp.where(valid, weight, 0.0)
                for c in range(3):
                    done[2 * c + half] = done[2 * c + half] + d[c] * weight
            return tuple(done)

        def chunk(number, total):
            first = number * CHUNK
            words = [words_ref[first + u, 16 * tile] for u in range(CHUNK)]
            seen = words[0]
            for word in words[1:]:
                seen = seen | word

            def fast(total):
                for u in range(CHUNK):
                    index = spread(nbr_ref[tile, pl.ds(first + u, 1), :])
                    high, low = lax.shift_right_logical(index, 7), index & 127
                    place = words[u] & 31
                    after = (place + 2) & 31
                    found = [take(table[place, g * 8:g * 8 + 8, :], low) for g in range(6)]
                    total = push(total, pull(found, high == 1, low, after), high < 2)
                return total

            def slow(total):
                def one(u, total):
                    index = spread(nbr_ref[tile, pl.ds(first + u, 1), :])
                    index = jnp.where(index == EMPTY, EMPTY, (index + (words_ref[first + u, 16 * tile] & 31) * 64) & 2047)
                    high, low = lax.shift_right_logical(index, 7), index & 127
                    found = lax.fori_loop(
                        0, 16, lambda place, found: tuple(pull(found, high == place, low, 2 * place)), tuple(own)
                    )
                    return push(total, found)

                return lax.fori_loop(0, CHUNK, one, total)

            def some(total):
                return lax.cond((seen & (1 << 8)) != 0, slow, fast, total)

            return lax.cond((seen & (1 << 9)) != 0, some, lambda total: total, total)

        zero = jnp.zeros((8, LANES), F32)
        total = lax.fori_loop(0, SLOTS // CHUNK, chunk, (zero,) * 6)
        for g in range(6):
            r = slice(g * 8, g * 8 + 8)
            momout_ref[r, at] = momout_ref[r, at] + kick_scale * total[g]
        leave(tile).start()
        return carry

    lax.fori_loop(0, TILES, atom_tile, 0)
    for out in outs:
        out.wait()
    for tile in range(TILES):
        leave(tile).wait()


def per_device(positions, momenta, thermostat, white_noise, drift_matrix, noise_matrix, leave_up, leave_down,
               ghost_up, ghost_down, neighbours):
    pos = positions.transpose(1, 0, 2).reshape(48, ATOMS)
    mom = momenta.transpose(1, 0, 2).reshape(48, ATOMS)
    therm = thermostat.transpose(0, 2, 1, 3).reshape(48, 8, ATOMS)
    noise = white_noise.transpose(1, 2, 0, 3).reshape(54, 8, ATOMS)
    drift = drift_matrix.transpose(1, 0, 2).reshape(144, 9)
    noisem = noise_matrix.transpose(1, 0, 2).reshape(144, 9)
    matrices, tables = jnp.asarray(MATRICES), jnp.asarray(TABLES)

    other_pos = shifted(pos, "bead", 1)
    other_mom = shifted(mom, "bead", 1)
    held = [pltpu.with_memory_space_constraint(x, pltpu.HBM) for x in (therm, noise, drift, noisem, neighbours)]
    q, therm, noise, coef, rows, words = call(
        kick_body,
        [
            struct(48, ATOMS + LANES), struct(48, 8, ATOMS), struct(54, 8, ATOMS), struct(288, 8, LANES),
            struct(TILES, SLOTS, LANES, dtype=I32), struct(SLOTS, LANES, dtype=I32),
        ],
        held, specs=[HBM] * 5,
        scratch=[
            pltpu.VMEM((144, 9), F32), pltpu.VMEM((144, 9), F32), pltpu.VMEM((SLOTS, ATOMS), I32),
            pltpu.SemaphoreType.DMA((2, TILES)), pltpu.SemaphoreType.DMA((3,)),
        ],
        flops=4000000, nbytes=3600000,
    )
    other_q = shifted(q, "bead", 1)
    modes, part = call(
        modes_body,
        [struct(3, 2, BEADS, ATOMS), struct(48, 8, LANES)],
        [leave_up, leave_down, pos, mom, other_pos, other_mom, matrices, therm, noise, coef],
        specs=[SMEM] * 2 + [VMEM] * 8,
        scratch=[pltpu.VMEM((48, 8, LANES), F32), pltpu.VMEM((54, 8, LANES), F32)],
        flops=8000000, nbytes=4000000,
    )
    bead_pos, bead_mom, mode_mom, up_buf, down_buf, up_pack, down_pack, codes = call(
        beads_body,
        [struct(48, ATOMS)] * 3 + [struct(264, LANES)] * 2 + [struct(8, LANES)] * 2 + [struct(8, LANES, dtype=I32)],
        [leave_up, leave_down, modes, q, other_q, matrices, tables, part, coef, ghost_up, ghost_down],
        specs=[SMEM] * 2 + [VMEM] * 9,
        scratch=[pltpu.VMEM((6, 8, LANES), F32)],
        flops=8000000, nbytes=2000000,
    )
    low = shifted(up_buf, "space", 1)
    low2 = shifted(up_pack, "space", 2)
    work = [therm, noise, mode_mom, coef]
    aux, down_buf, down_pack = call(
        aux_first, [struct(48, 8, ATOMS), struct(264, LANES), struct(8, LANES)], work + [down_buf, down_pack],
        specs=[VMEM] * 4 + [ANY] * 2, out_specs=[VMEM, ANY, ANY], alias={4: 1, 5: 2}, flops=1000, nbytes=1000,
    )
    high = shifted(down_buf, "space", -1)
    high2 = shifted(down_pack, "space", -2)
    (aux,) = call(aux_second, [struct(48, 8, ATOMS)], [aux] + work, alias={0: 0}, flops=16000000, nbytes=5000000)
    moved, slab, out_aux = call(
        force_body,
        [struct(48, ATOMS), struct(48, ATOMS), struct(48, 8, ATOMS)],
        [words, codes, rows, bead_pos, bead_mom, aux, up_pack, low, high, low2, high2],
        out_specs=[HBM] * 3,
        scratch=[
            pltpu.VMEM((WINDOWS, 48, LANES), F32),
            pltpu.VMEM((48, 8, ATOMS), F32),
            pltpu.VMEM((48, ATOMS), F32),
            pltpu.VMEM((48, ATOMS), F32),
            pltpu.VMEM((60, 8, LANES), F32),
            pltpu.SMEM((SLOTS, LANES), I32),
            pltpu.SemaphoreType.DMA((3,)),
            pltpu.SemaphoreType.DMA((TILES,)),
        ],
        flops=30000000, nbytes=4000000,
    )
    moved = moved.reshape(3, HALF, ATOMS).transpose(1, 0, 2)
    slab = slab.reshape(3, HALF, ATOMS).transpose(1, 0, 2)
    out_aux = out_aux.reshape(HALF, 3, 8, ATOMS).transpose(0, 2, 1, 3)
    return (moved, slab, out_aux)


def solution(mesh):
    in_specs = (
        P("bead", None, "space"),
        P("bead", None, "space"),
        P("bead", None, None, "space"),
        P("bead", None, None, "space"),
        P("bead", None, None),
        P("bead", None, None),
        P("space"),
        P("space"),
        P("space"),
        P("space"),
        P(None, "space"),
    )
    out_specs = (P("bead", None, "space"), P("bead", None, "space"), P("bead", None, None, "space"))

    return jax.shard_map(per_device, mesh=mesh, in_specs=in_specs, out_specs=out_specs, check_vma=False)
```
